256 devices in a mesh: depth: 32 (over z, x_hi, core), shot: 8 (over y, x_lo).
Axes of the slice: x: 4 (x_hi: 2, x_lo: 2; x = x_hi * 2 + x_lo), y: 4, z: 8, core: 2. Of those that a mesh axis runs over, the one named last changes fastest.
Arguments:
- courant: float32 [512, 64, 128], P('depth'), may hold values from 0.04 to 0.2
- wave_before: float32 [8, 512, 64, 128], P('shot', 'depth'), may hold values from -10 to 10
- wave_current: float32 [8, 512, 64, 128], P('shot', 'depth'), may hold values from -10 to 10
- adjoint_after: float32 [8, 512, 64, 128], P('shot', 'depth'), may hold values from -10 to 10
- adjoint_current: float32 [8, 512, 64, 128], P('shot', 'depth'), may hold values from -10 to 10
- source_cell: int32 [8], P('shot'), may hold values from 0 to 4194303
- wavelet: float32 [8, 4], P('shot'), may hold values from -15 to 15
- receiver_cell: int32 [8, 256], P('shot'), may hold values from 0 to 4194303
- residual: float32 [8, 4, 256], P('shot'), may hold values from -12 to 12
- history: float32 [2, 5, 512, 64, 128], P(None, None, 'depth', 'shot'), may hold values from -23 to 23, as said below
Outputs:
- gradient: float32 [512, 64, 128], P('depth', 'shot')
- direction: float32 [512, 64, 128], P('depth', 'shot')
- courant_next: float32 [512, 64, 128], P('depth')
The draws below stay inside these ranges and needn't reach their ends.
Inputs may be any that keep to these rules, and one draw needn't show every extreme that they name: In every pair the sum over all cells of history[0] times history[1] is positive.
All inputs are finite; a program needn't handle non-finite values.
Results may differ from the reference program's by a relative error of at most 0.00026.
Values sent between devices are 32-bit elements; how exact they have to be, the bound alone decides.
A program may use at most 128 MiB of HBM per device.

```python
import math
import jax
import jax.numpy as jnp

NX = 64
NY = 128
RECV = 256
STEPS = 4
PAIRS = 5
SHOTS = 8
NZ = 512


def shared_pattern(key):
    base = jax.random.fold_in(key, 7001)
    key_sign, key_phase, key_amp = jax.random.split(base, 3)
    signs = jax.random.randint(key_sign, (SHOTS, 3), 0, 2) * 2 - 1
    phase = jax.random.uniform(key_phase, (SHOTS, 1, 1, 1), jnp.float32, -math.pi, math.pi)
    amplitude = jax.random.uniform(key_amp, (SHOTS, 1, 1, 1), jnp.float32, 2.5, 3.5)
    depth_index = jnp.arange(NZ, dtype=jnp.int32)[None, :, None, None]
    across_index = jnp.arange(NX, dtype=jnp.int32)[None, None, :, None]
    along_index = jnp.arange(NY, dtype=jnp.int32)[None, None, None, :]
    sign_depth = signs[:, 0][:, None, None, None]
    sign_across = signs[:, 1][:, None, None, None]
    sign_along = signs[:, 2][:, None, None, None]
    cycle = (sign_depth * depth_index + sign_across * across_index + sign_along * along_index + 1024) % 16
    angle = cycle.astype(jnp.float32) * (2.0 * math.pi / 16.0) + phase
    return amplitude * jnp.cos(angle)


def rough_part(key, label):
    sub_key = jax.random.fold_in(key, label)
    array_shape = (SHOTS, NZ, NX, NY)
    return jnp.clip(jax.random.normal(sub_key, array_shape, jnp.float32), -6.0, 6.0)


def draw_wave_before(key, part):
    return (shared_pattern(key) + rough_part(key, 8101)).astype(jnp.float32)


def draw_wave_current(key, part):
    return (shared_pattern(key) + rough_part(key, 8102)).astype(jnp.float32)


def draw_adjoint_after(key, part):
    return (shared_pattern(key) + rough_part(key, 8103)).astype(jnp.float32)


def draw_adjoint_current(key, part):
    return (shared_pattern(key) + rough_part(key, 8104)).astype(jnp.float32)


def draw_history(key, part):
    key_steps, key_factor, key_offset = jax.random.split(key, 3)
    array_shape = (PAIRS, NZ, NX, NY)
    offsets = jax.random.uniform(key_offset, (PAIRS, 1, 1, 1), jnp.float32, 0.6, 1.4)
    noise = jnp.clip(jax.random.normal(key_steps, array_shape, jnp.float32), -6.0, 6.0)
    displaced = offsets + noise
    factor = jnp.exp(jax.random.uniform(key_factor, array_shape, jnp.float32, math.log(0.3), math.log(3.0)))
    return jnp.stack([displaced, displaced * factor]).astype(jnp.float32)


def set_ends(drawn, rng, smallest, largest):
    dims = drawn.shape
    spot = [jax.random.randint(jax.random.fold_in(rng, axis), (), 0, dims[axis]) for axis in range(len(dims))]
    drawn = drawn.at[tuple(spot)].set(smallest)
    longest = dims.index(max(dims))
    spot[longest] = (spot[longest] + 1) % dims[longest]
    return drawn.at[tuple(spot)].set(largest)


def level_of(stream_key, shape, cuts, low, largest):
    def one(dim, shards_of):
        draws = jax.random.uniform(jax.random.fold_in(jax.random.fold_in(stream_key, 6), dim), (shards_of,), jnp.float32, low / len(cuts), largest / len(cuts))
        return jnp.repeat(jnp.exp(draws), shape[dim] // shards_of).reshape((-1,) + (1,) * (len(shape) - dim - 1))

    loudness = one(*cuts[0])
    for cut in cuts[1:]:
        loudness = loudness * one(*cut)
    return loudness


def bell_draw(own_key, extent, scale, limit, shards=(), held_as=jnp.bfloat16):
    result = scale * jax.random.normal(own_key, extent, jnp.float32)
    if shards:
        result = result * level_of(own_key, extent, shards, -0.22, 0.18)
    return jnp.clip(result, -limit, limit).astype(held_as)


def setup_inputs(seed: int = 0) -> dict:
    keys = jax.random.split(jax.random.key(seed), 11)
    return {
        "courant": jnp.clip(jnp.exp(math.log(0.2) - 1.609438 * jax.random.uniform(keys[0], (NZ, NX, NY), jnp.float32) ** level_of(keys[0], (NZ, NX, NY), ((0, 32),), -0.2, 0.2)), 0.04, 0.2),
        "wave_before": draw_wave_before(jax.random.fold_in(keys[10], 71), 0),
        "wave_current": draw_wave_current(jax.random.fold_in(keys[10], 71), 0),
        "adjoint_after": draw_adjoint_after(jax.random.fold_in(keys[10], 71), 0),
        "adjoint_current": draw_adjoint_current(jax.random.fold_in(keys[10], 71), 0),
        "source_cell": set_ends(jax.random.randint(keys[5], (SHOTS,), 0, NZ * NX * NY), jax.random.fold_in(keys[5], 1), 0, (NZ * NX * NY) - 1).astype(jnp.int32),
        "wavelet": bell_draw(keys[6], (SHOTS, STEPS), 5.0, 15.0, ((0, 8),), jnp.float32),
        "receiver_cell": set_ends(jax.random.randint(keys[7], (SHOTS, RECV), 0, NZ * NX * NY), jax.random.fold_in(keys[7], 1), 0, (NZ * NX * NY) - 1).astype(jnp.int32),
        "residual": bell_draw(keys[8], (SHOTS, STEPS, RECV), 3.0, 12.0, ((0, 8),), jnp.float32),
        "history": draw_history(jax.random.fold_in(keys[10], 71), 0),
    }


coefficients = (-205.0 / 72.0, 8.0 / 5.0, -1.0 / 5.0, 8.0 / 315.0, -1.0 / 560.0)


def laplace_core(extended):
    interior = extended[4:-4]
    count_rows = interior.shape[0]
    width_x = interior.shape[1]
    width_y = interior.shape[2]
    padded = jnp.pad(interior, ((0, 0), (4, 4), (4, 4)))
    summed = (3.0 * coefficients[0]) * interior
    for reach in range(1, 5):
        weight = coefficients[reach]
        summed = summed + weight * (extended[4 + reach:4 + reach + count_rows] + extended[4 - reach:4 - reach + count_rows])
        summed = summed + weight * (padded[:, 4 + reach:4 + reach + width_x, 4:4 + width_y] + padded[:, 4 - reach:4 - reach + width_x, 4:4 + width_y])
        summed = summed + weight * (padded[:, 4:4 + width_x, 4 + reach:4 + reach + width_y] + padded[:, 4:4 + width_x, 4 - reach:4 - reach + width_y])
    return summed


def inject(volume, cell_ids, values, offset):
    count_rows = volume.shape[0]
    plane_size = volume.shape[1] * volume.shape[2]
    depth_row = cell_ids // plane_size - offset
    remainder = cell_ids % plane_size
    inside = (depth_row >= 0) & (depth_row < count_rows)
    row_safe = jnp.clip(depth_row, 0, count_rows - 1)
    return volume.at[row_safe, remainder // volume.shape[2], remainder % volume.shape[2]].add(jnp.where(inside, values, jnp.zeros_like(values)))


def depth_pad(volume):
    return jnp.pad(volume, ((4, 4), (0, 0), (0, 0)))


def reference(courant, wave_before, wave_current, adjoint_after, adjoint_current, source_cell, wavelet, receiver_cell, residual, history):
    summed = jnp.zeros(courant.shape, jnp.float32)
    zero_offset = jnp.int32(0)
    for shot_num in range(SHOTS):
        wave_old = wave_before[shot_num]
        wave_now = wave_current[shot_num]
        laplacians = []
        for moment in range(STEPS):
            laplacian = laplace_core(depth_pad(wave_now))
            wave_new = 2.0 * wave_now - wave_old + courant * laplacian
            wave_new = inject(wave_new, source_cell[shot_num:shot_num + 1], wavelet[shot_num, moment:moment + 1], zero_offset)
            laplacians.append(laplacian)
            wave_old, wave_now = wave_now, wave_new
        adjoint_old = adjoint_after[shot_num]
        adjoint_now = adjoint_current[shot_num]
        for moment in reversed(range(STEPS)):
            adjoint_new = 2.0 * adjoint_now - adjoint_old + laplace_core(depth_pad(courant * adjoint_now))
            adjoint_new = inject(adjoint_new, receiver_cell[shot_num], residual[shot_num, moment], zero_offset)
            summed = summed + adjoint_new * laplacians[moment]
            adjoint_old, adjoint_now = adjoint_now, adjoint_new
    gradient = summed * (1.0 / (SHOTS * STEPS))
    displaced = history[0]
    changes = history[1]
    curvature = [jnp.sum(displaced[number] * changes[number]) for number in range(PAIRS)]
    inverse = [1.0 / value_sy for value_sy in curvature]
    search = gradient
    alphas = [None] * PAIRS
    for number in reversed(range(PAIRS)):
        alphas[number] = inverse[number] * jnp.sum(displaced[number] * search)
        search = search - alphas[number] * changes[number]
    scaled = (curvature[PAIRS - 1] / jnp.sum(changes[PAIRS - 1] * changes[PAIRS - 1])) * search
    for number in range(PAIRS):
        correction = inverse[number] * jnp.sum(changes[number] * scaled)
        scaled = scaled + (alphas[number] - correction) * displaced[number]
    direction = -scaled
    courant_next = courant + 0.05 * direction
    return (gradient, direction, courant_next)
```

```python
import jax
import jax.numpy as jnp
from jax import lax
from jax.sharding import PartitionSpec as P

STEPS = 4
PAIRS = 5


coefficients = (-205.0 / 72.0, 8.0 / 5.0, -1.0 / 5.0, 8.0 / 315.0, -1.0 / 560.0)


def with_halo(cells, sides, width):
    for axis, dim in sides:
        count = lax.axis_size(axis)
        ends = count - 1
        head = lax.slice_in_dim(cells, 0, width, axis=dim)
        tail = lax.slice_in_dim(cells, cells.shape[dim] - width, cells.shape[dim], axis=dim)
        cells = jnp.concatenate(
            [
                lax.ppermute(tail, axis, [(i, (i + 1) % count) for i in range(ends)]),
                cells,
                lax.ppermute(head, axis, [((i + 1) % count, i) for i in range(ends)]),
            ],
            axis=dim,
        )
    return cells


def laplace_core(extended):
    interior = extended[4:-4]
    count_rows = interior.shape[0]
    width_x = interior.shape[1]
    width_y = interior.shape[2]
    padded = jnp.pad(interior, ((0, 0), (4, 4), (4, 4)))
    summed = 3.0 * coefficients[0] * interior
    for reach in range(1, 5):
        weight = coefficients[reach]
        summed = summed + weight * (
            extended[4 + reach : 4 + reach + count_rows]
            + extended[4 - reach : 4 - reach + count_rows]
        )
        summed = summed + weight * (
            padded[:, 4 + reach : 4 + reach + width_x, 4 : 4 + width_y]
            + padded[:, 4 - reach : 4 - reach + width_x, 4 : 4 + width_y]
        )
        summed = summed + weight * (
            padded[:, 4 : 4 + width_x, 4 + reach : 4 + reach + width_y]
            + padded[:, 4 : 4 + width_x, 4 - reach : 4 - reach + width_y]
        )
    return summed


def inject(volume, cell_ids, values, offset):
    count_rows = volume.shape[0]
    plane_size = volume.shape[1] * volume.shape[2]
    depth_row = cell_ids // plane_size - offset
    remainder = cell_ids % plane_size
    inside = (depth_row >= 0) & (depth_row < count_rows)
    row_safe = jnp.clip(depth_row, 0, count_rows - 1)
    return volume.at[row_safe, remainder // volume.shape[2], remainder % volume.shape[2]].add(
        jnp.where(inside, values, jnp.zeros_like(values))
    )


def per_device(
    courant,
    wave_before,
    wave_current,
    adjoint_after,
    adjoint_current,
    source_cell,
    wavelet,
    receiver_cell,
    residual,
    history,
):
    slab_rows = courant.shape[0]
    first_row = lax.axis_index("depth") * slab_rows
    shot_count = lax.axis_size("shot")
    summed = jnp.zeros(courant.shape, jnp.float32)
    laplacians = []
    wave_old = wave_before[0]
    wave_now = wave_current[0]
    for moment in range(STEPS):
        extended = with_halo(wave_now, (("depth", 0),), 4)
        laplacian = laplace_core(extended)
        wave_new = 2.0 * wave_now - wave_old + courant * laplacian
        wave_new = inject(wave_new, source_cell, wavelet[0, moment : moment + 1], first_row)
        laplacians.append(laplacian)
        wave_old, wave_now = (wave_now, wave_new)
    adjoint_old = adjoint_after[0]
    adjoint_now = adjoint_current[0]
    for moment in reversed(range(STEPS)):
        extended = with_halo(courant * adjoint_now, (("depth", 0),), 4)
        adjoint_new = 2.0 * adjoint_now - adjoint_old + laplace_core(extended)
        adjoint_new = inject(adjoint_new, receiver_cell[0], residual[0, moment], first_row)
        summed = summed + adjoint_new * laplacians[moment]
        adjoint_old, adjoint_now = (adjoint_now, adjoint_new)
    grad_piece = lax.psum_scatter(summed, "shot", scatter_dimension=1, tiled=True) * (
        1.0 / (shot_count * STEPS)
    )
    displaced = history[0]
    changes = history[1]
    step_change = jnp.einsum("izxy,jzxy->ij", displaced, changes, precision=lax.Precision.HIGHEST)
    change_change = jnp.einsum("izxy,jzxy->ij", changes, changes, precision=lax.Precision.HIGHEST)
    step_grad = jnp.sum(displaced * grad_piece, axis=(1, 2, 3))
    change_grad = jnp.sum(changes * grad_piece, axis=(1, 2, 3))
    packed = jnp.concatenate(
        [step_change, change_change, step_grad[None], change_grad[None]], axis=0
    )
    packed = lax.psum(packed, ("depth", "shot"))
    step_change = packed[:PAIRS]
    change_change = packed[PAIRS : 2 * PAIRS]
    step_grad = packed[2 * PAIRS]
    change_grad = packed[2 * PAIRS + 1]
    inverse = [1.0 / step_change[i, i] for i in range(PAIRS)]
    alphas = [None] * PAIRS
    for i in reversed(range(PAIRS)):
        value = step_grad[i]
        for j in range(i + 1, PAIRS):
            value = value - alphas[j] * step_change[i, j]
        alphas[i] = inverse[i] * value
    gamma = step_change[PAIRS - 1, PAIRS - 1] / change_change[PAIRS - 1, PAIRS - 1]
    gains = []
    for i in range(PAIRS):
        value = change_grad[i]
        for j in range(PAIRS):
            value = value - alphas[j] * change_change[i, j]
        value = gamma * value
        for j in range(i):
            value = value + gains[j] * step_change[j, i]
        gains.append(alphas[i] - inverse[i] * value)
    scaled = grad_piece
    for i in range(PAIRS):
        scaled = scaled - alphas[i] * changes[i]
    scaled = gamma * scaled
    for i in range(PAIRS):
        scaled = scaled + gains[i] * displaced[i]
    direction = -scaled
    piece_width = grad_piece.shape[1]
    own_courant = lax.dynamic_slice_in_dim(
        courant, lax.axis_index("shot") * piece_width, piece_width, 1
    )
    next_piece = own_courant + 0.05 * direction
    courant_next = lax.all_gather(next_piece, "shot", axis=1, tiled=True)
    return (grad_piece, direction, courant_next)


def solution(mesh):
    return jax.shard_map(
        per_device,
        mesh=mesh,
        in_specs=(
            P("depth", None, None),
            P("shot", "depth", None, None),
            P("shot", "depth", None, None),
            P("shot", "depth", None, None),
            P("shot", "depth", None, None),
            P("shot"),
            P("shot", None),
            P("shot", None),
            P("shot", None, None),
            P(None, None, "depth", "shot", None),
        ),
        out_specs=(P("depth", "shot", None), P("depth", "shot", None), P("depth", None, None)),
        check_vma=False,
    )
```

```python
import functools

import jax
import jax.numpy as jnp
from jax import lax
from jax.experimental import pallas as pl
from jax.experimental.pallas import tpu as pltpu
from jax.sharding import PartitionSpec as P

STEPS = 4
PAIRS = 5
REACH = 4
PAD = 8
MESH = pl.DeviceIdType.MESH

coefficients = (-205.0 / 72.0, 8.0 / 5.0, -1.0 / 5.0, 8.0 / 315.0, -1.0 / 560.0)


def kernel(
    depth_count,
    shot_count,
    inner_count,
    source_ref,
    wavelet_ref,
    receiver_ref,
    residual_ref,
    courant_hbm,
    before_hbm,
    current_hbm,
    after_hbm,
    adjoint_hbm,
    history_hbm,
    gradient_out,
    direction_out,
    next_out,
    wave,
    scaled_adj,
    lap,
    adj,
    before,
    after,
    courant,
    history,
    inject,
    terms,
    parts,
    gram,
    next_piece,
    slots_shot,
    slots_inner,
    slots_outer,
    load_sem,
    halo_send,
    halo_recv,
    part_send,
    part_recv,
    shot_send,
    shot_recv,
    inner_send,
    inner_recv,
    outer_send,
    outer_recv,
    next_send,
    next_recv,
    next_local,
):
    rows, width, lanes = courant.shape
    here = lax.axis_index("depth")
    me = lax.axis_index("shot")
    outer_count = depth_count // inner_count
    inner_me = lax.rem(here, inner_count)
    outer_me = lax.div(here, inner_count)
    piece = width // shot_count
    first = 0
    last = depth_count - 1

    def shot_peer(step):
        return lax.rem(me + step, shot_count)

    def inner_peer(step):
        return lax.rem(inner_me + step, inner_count)

    def outer_peer(step):
        return lax.rem(outer_me + step, outer_count)

    def depth_of(outer, inner):
        return outer * inner_count + inner

    barrier = pltpu.get_barrier_semaphore()

    def greet(depth, shot):
        pl.semaphore_signal(barrier, inc=1, device_id=(depth, shot), device_id_type=MESH)

    greet(lax.rem(here + 1, depth_count), me)
    greet(lax.rem(here + depth_count - 1, depth_count), me)
    for step in range(1, inner_count):
        greet(depth_of(outer_me, inner_peer(step)), me)
    for step in range(1, outer_count):
        greet(depth_of(outer_peer(step), inner_me), me)
    for step in range(1, shot_count):
        greet(here, shot_peer(step))
    greetings = 2 + (inner_count - 1) + (outer_count - 1) + (shot_count - 1)

    inside = pl.ds(REACH, rows)
    across = pl.ds(PAD, width)
    loads = [
        pltpu.make_async_copy(courant_hbm, courant, load_sem.at[0]),
        pltpu.make_async_copy(adjoint_hbm.at[0], adj.at[0], load_sem.at[1]),
        pltpu.make_async_copy(current_hbm.at[0], wave.at[0, inside, across], load_sem.at[2]),
        pltpu.make_async_copy(before_hbm.at[0], before, load_sem.at[3]),
        pltpu.make_async_copy(after_hbm.at[0], after, load_sem.at[4]),
        pltpu.make_async_copy(history_hbm, history, load_sem.at[5]),
    ]
    for load in loads:
        load.start()

    pads = jnp.zeros((rows, PAD, lanes), jnp.float32)
    for field in (wave, scaled_adj):
        for moment in range(STEPS):
            field[moment, pl.ds(REACH, rows), pl.ds(0, PAD), :] = pads
            field[moment, pl.ds(REACH, rows), pl.ds(PAD + width, PAD), :] = pads
    outside = jnp.zeros((REACH, width, lanes), jnp.float32)

    @pl.when(here == first)
    def _():
        for field in (wave, scaled_adj):
            for moment in range(STEPS):
                field[moment, pl.ds(0, REACH), across, :] = outside

    @pl.when(here == last)
    def _():
        for field in (wave, scaled_adj):
            for moment in range(STEPS):
                field[moment, pl.ds(REACH + rows, REACH), across, :] = outside

    def halo_copy(field, number, moment, up, source=None):
        if source is None:
            start = REACH if up else rows
            source = field.at[moment, pl.ds(start, REACH), across]
        target = field.at[moment, pl.ds(REACH + rows if up else 0, REACH), across]
        side = 0 if up else 1
        to = here - 1 if up else here + 1
        return pltpu.make_async_remote_copy(
            src_ref=source,
            dst_ref=target,
            send_sem=halo_send.at[number, moment, side],
            recv_sem=halo_recv.at[number, moment, side],
            device_id=(to, me),
            device_id_type=MESH,
        )

    def send_halo(field, number, moment, up, source=None):
        @pl.when(here > first if up else here < last)
        def _():
            halo_copy(field, number, moment, up, source).start()

    def wait_halo(field, number, moment, above):
        @pl.when(here > first if above else here < last)
        def _():
            halo_copy(field, number, moment, not above).wait_recv()

    pl.semaphore_wait(barrier, greetings)

    send_halo(wave, 0, 0, True, current_hbm.at[0, pl.ds(0, REACH)])
    send_halo(wave, 0, 0, False, current_hbm.at[0, pl.ds(rows - REACH, REACH)])

    loads[0].wait()
    loads[1].wait()

    def first_scaled(z):
        scaled_adj[0, z + REACH, across, :] = courant[z] * adj[0, z]

    def planes(low, high, body):
        def one(z, carry):
            body(z)
            return carry

        lax.fori_loop(low, high, one, 0)

    planes(0, REACH, first_scaled)
    send_halo(scaled_adj, 1, 0, True)
    planes(rows - REACH, rows, first_scaled)
    send_halo(scaled_adj, 1, 0, False)
    planes(REACH, rows - REACH, first_scaled)

    lane_bits = lanes.bit_length() - 1
    cells = receiver_ref[...]
    count = cells.shape[1]
    cell_rows = lax.shift_right_logical(cells, lane_bits) - here * (rows * width)
    cell_lanes = cells & (lanes - 1)
    lane_hit = lax.broadcasted_iota(jnp.int32, (lanes, count), 0) == cell_lanes
    block = 4 * width
    weights = []
    for moment in range(STEPS):
        value = jnp.where(lane_hit, residual_ref[0, moment : moment + 1, :], 0.0)
        high = value.astype(jnp.bfloat16)
        rest = value - high.astype(jnp.float32)
        middle = rest.astype(jnp.bfloat16)
        low = (rest - middle.astype(jnp.float32)).astype(jnp.bfloat16)
        weights.append((high, middle, low))

    def inject_block(number, carry):
        ids = lax.broadcasted_iota(jnp.int32, (block, count), 0) + number * block
        hit = jnp.where(ids == cell_rows, 1.0, 0.0).astype(jnp.bfloat16)
        for moment in range(STEPS):
            total = None
            for weight in reversed(weights[moment]):
                product = lax.dot_general(
                    hit, weight, (((1,), (1,)), ((), ())), preferred_element_type=jnp.float32
                )
                total = product if total is None else total + product
            inject[moment, pl.ds(number * 4, 4)] = total.reshape(4, width, lanes)
        return carry

    lax.fori_loop(0, rows // 4, inject_block, 0)

    source = source_ref[0]
    plane_ids = lax.broadcasted_iota(jnp.int32, (width, lanes), 0) * lanes
    plane_ids = plane_ids + lax.broadcasted_iota(jnp.int32, (width, lanes), 1)
    lane_ids = lax.broadcasted_iota(jnp.int32, (width, lanes), 1)

    def laplace(field, moment, z):
        at = z + REACH
        center = field[moment, at, across, :]
        total = (3.0 * coefficients[0]) * center
        for reach in range(1, REACH + 1):
            ahead = jnp.where(lane_ids < lanes - reach, pltpu.roll(center, lanes - reach, 1), 0.0)
            behind = jnp.where(lane_ids >= reach, pltpu.roll(center, reach, 1), 0.0)
            depth = field[moment, at + reach, across, :] + field[moment, at - reach, across, :]
            side = (
                field[moment, at, pl.ds(PAD + reach, width), :]
                + field[moment, at, pl.ds(PAD - reach, width), :]
            )
            total = total + coefficients[reach] * (depth + side + (ahead + behind))
        return center, total

    def forward_plane(moment, z):
        center, total = laplace(wave, moment, z)
        lap[moment, z] = total
        if moment < STEPS - 1:
            old = before[z] if moment == 0 else wave[moment - 1, z + REACH, across, :]
            new = 2.0 * center - old + courant[z] * total
            offset = source - (here * rows + z) * (width * lanes)
            new = new + jnp.where(plane_ids == offset, wavelet_ref[0, moment], 0.0)
            wave[moment + 1, z + REACH, across, :] = new

    def adjoint_plane(moment, z):
        _, total = laplace(scaled_adj, moment, z)
        old = after[z] if moment == 0 else adj[moment - 1, z]
        new = 2.0 * adj[moment, z] - old + total + inject[STEPS - 1 - moment, z]
        if moment < STEPS - 1:
            adj[moment + 1, z] = new
            scaled_adj[moment + 1, z + REACH, across, :] = courant[z] * new
        else:
            total = new * lap[0, z]
            for number in range(1, STEPS):
                total = total + adj[number, z] * lap[STEPS - number, z]
            terms[:, z] = total.reshape(shot_count, piece, lanes)

    stretches = ((REACH, rows - 2 * REACH), (0, REACH), (rows - REACH, REACH))

    def part_copy(number, peer, slot):
        start, length = stretches[number]
        return pltpu.make_async_remote_copy(
            src_ref=terms.at[peer, pl.ds(start, length)],
            dst_ref=parts.at[slot, pl.ds(start, length)],
            send_sem=part_send.at[number, peer],
            recv_sem=part_recv.at[number, slot],
            device_id=(here, peer),
            device_id_type=MESH,
        )

    def send_parts(number):
        for step in range(1, shot_count):
            part_copy(number, shot_peer(step), me).start()

    loads[2].wait()
    loads[3].wait()
    loads[4].wait()
    for moment in range(STEPS):
        more = moment < STEPS - 1
        planes(REACH, rows - REACH, functools.partial(forward_plane, moment))
        planes(REACH, rows - REACH, functools.partial(adjoint_plane, moment))
        if not more:
            send_parts(0)
        if moment == 0:
            loads[5].wait()
            pairs = [(0, i, j) for j in range(PAIRS) for i in range(j + 1)]
            pairs += [(1, i, j) for j in range(PAIRS) for i in range(j + 1)]

            def gram_plane(z, sums):
                held = [[history[kind, i, z] for i in range(PAIRS)] for kind in range(2)]
                return tuple(
                    total + held[kind][i] * held[1][j]
                    for total, (kind, i, j) in zip(sums, pairs)
                )

            sums = lax.fori_loop(
                0, rows, gram_plane, tuple(jnp.zeros((piece, lanes), jnp.float32) for _ in pairs)
            )
            row_lane = lax.broadcasted_iota(jnp.int32, (1, lanes), 1)
            packed = jnp.zeros((1, lanes), jnp.float32)
            for total, (kind, i, j) in zip(sums, pairs):
                value = jnp.sum(jnp.sum(total, axis=0, keepdims=True), axis=1, keepdims=True)
                spots = [(2 + PAIRS * kind + j) * 8 + i]
                if kind == 1 and i != j:
                    spots.append((2 + PAIRS * kind + i) * 8 + j)
                for spot in spots:
                    packed = jnp.where(row_lane == spot, value, packed)
            gram[...] = packed
        wait_halo(wave, 0, moment, True)
        planes(0, REACH, functools.partial(forward_plane, moment))
        if more:
            send_halo(wave, 0, moment + 1, True)
        wait_halo(wave, 0, moment, False)
        planes(rows - REACH, rows, functools.partial(forward_plane, moment))
        if more:
            send_halo(wave, 0, moment + 1, False)
        wait_halo(scaled_adj, 1, moment, True)
        planes(0, REACH, functools.partial(adjoint_plane, moment))
        if more:
            send_halo(scaled_adj, 1, moment + 1, True)
        else:
            send_parts(1)
        wait_halo(scaled_adj, 1, moment, False)
        planes(rows - REACH, rows, functools.partial(adjoint_plane, moment))
        if more:
            send_halo(scaled_adj, 1, moment + 1, False)
        else:
            send_parts(2)

    for number in range(len(stretches)):
        for step in range(1, shot_count):
            part_copy(number, me, shot_peer(step)).wait_recv()

    scale = 1.0 / (shot_count * STEPS)

    def own_plane(z, sums):
        total = terms[me, z]
        for step in range(1, shot_count):
            total = total + parts[shot_peer(step), z]
        total = total * scale
        gradient_out[z] = total
        return tuple(
            held + history[number // PAIRS, number % PAIRS, z] * total
            for number, held in enumerate(sums)
        )

    sums = lax.fori_loop(
        0, rows, own_plane, tuple(jnp.zeros((piece, lanes), jnp.float32) for _ in range(2 * PAIRS))
    )
    row_lane = lax.broadcasted_iota(jnp.int32, (1, lanes), 1)
    packed = gram[...]
    for number, total in enumerate(sums):
        value = jnp.sum(jnp.sum(total, axis=0, keepdims=True), axis=1, keepdims=True)
        spot = (number // PAIRS) * 8 + number % PAIRS
        packed = jnp.where(row_lane == spot, value, packed)

    def gather_sum(value, slots, send, recv, mine, number, peer_of, device_of):
        slots[mine] = value

        def one(peer, slot):
            return pltpu.make_async_remote_copy(
                src_ref=slots.at[mine],
                dst_ref=slots.at[slot],
                send_sem=send.at[peer],
                recv_sem=recv.at[slot],
                device_id=device_of(peer),
                device_id_type=MESH,
            )

        for step in range(1, number):
            one(peer_of(step), mine).start()
        for step in range(1, number):
            one(mine, peer_of(step)).wait_recv()
        total = slots[0]
        for slot in range(1, number):
            total = total + slots[slot]
        for step in range(1, number):
            one(peer_of(step), mine).wait_send()
        return total

    packed = gather_sum(
        packed, slots_shot, shot_send, shot_recv, me, shot_count,
        shot_peer, lambda peer: (here, peer),
    )
    packed = gather_sum(
        packed, slots_inner, inner_send, inner_recv, inner_me, inner_count,
        inner_peer, lambda peer: (depth_of(outer_me, peer), me),
    )
    packed = gather_sum(
        packed, slots_outer, outer_send, outer_recv, outer_me, outer_count,
        outer_peer, lambda peer: (depth_of(peer, inner_me), me),
    )

    spread = jnp.broadcast_to(packed, (8, lanes))
    sub = lax.broadcasted_iota(jnp.int32, (8, lanes), 0)
    lane = lax.broadcasted_iota(jnp.int32, (8, lanes), 1)

    def column(spots):
        return jnp.broadcast_to(
            jnp.sum(jnp.where(lane == spots, spread, 0.0), axis=1, keepdims=True), (8, lanes)
        )

    step_grad = column(sub)
    change_grad = column(8 + sub)
    step_change = [column((2 + j) * 8 + sub) for j in range(PAIRS)]
    step_change_row = [column((2 + sub) * 8 + i) for i in range(PAIRS)]
    change_change = [column((2 + PAIRS + j) * 8 + sub) for j in range(PAIRS)]
    curvature = jnp.where(sub < PAIRS, column((2 + sub) * 8 + sub), 1.0)
    inverse = 1.0 / curvature

    def entry(value, i):
        return jnp.broadcast_to(value[i : i + 1, :], (8, lanes))

    alphas = [None] * PAIRS
    running = step_grad
    for i in reversed(range(PAIRS)):
        alphas[i] = entry(inverse * running, i)
        running = running - alphas[i] * step_change[i]
    gamma = entry(curvature, PAIRS - 1) / entry(change_change[PAIRS - 1], PAIRS - 1)
    running = change_grad
    for j in range(PAIRS):
        running = running - alphas[j] * change_change[j]
    running = gamma * running
    gains = []
    for i in range(PAIRS):
        gain = alphas[i] - entry(inverse * running, i)
        gains.append(gain)
        running = running + gain * step_change_row[i]

    own_lateral = pl.ds(pl.multiple_of(me * piece, piece), piece)

    def direction_plane(z, carry):
        search = gradient_out[z]
        for i in range(PAIRS):
            search = search - alphas[i] * history[1, i, z]
        search = gamma * search
        for i in range(PAIRS):
            search = search + gains[i] * history[0, i, z]
        direction_out[z] = -search
        next_piece[z] = courant[z, own_lateral, :] - 0.05 * search
        return carry

    lax.fori_loop(0, rows, direction_plane, 0)

    def next_copy(peer, slot):
        spot = pl.ds(pl.multiple_of(slot * piece, piece), piece)
        return pltpu.make_async_remote_copy(
            src_ref=next_piece,
            dst_ref=next_out.at[:, spot],
            send_sem=next_send.at[peer],
            recv_sem=next_recv.at[slot],
            device_id=(here, peer),
            device_id_type=MESH,
        )

    for step in range(1, shot_count):
        next_copy(shot_peer(step), me).start()
    own = pltpu.make_async_copy(next_piece, next_out.at[:, own_lateral], next_local)
    own.start()

    for number, field in enumerate((wave, scaled_adj)):
        for moment in range(STEPS):
            for up in (True, False):

                @pl.when(here > first if up else here < last)
                def _():
                    halo_copy(field, number, moment, up).wait_send()

    for number in range(len(stretches)):
        for step in range(1, shot_count):
            part_copy(number, shot_peer(step), me).wait_send()
    own.wait()
    for step in range(1, shot_count):
        next_copy(me, shot_peer(step)).wait_recv()
    for step in range(1, shot_count):
        next_copy(shot_peer(step), me).wait_send()


def per_device(
    courant,
    wave_before,
    wave_current,
    adjoint_after,
    adjoint_current,
    source_cell,
    wavelet,
    receiver_cell,
    residual,
    history,
):
    depth_count = lax.axis_size("depth")
    shot_count = lax.axis_size("shot")
    inner_count = 4
    outer_count = depth_count // inner_count
    rows, width, lanes = courant.shape
    piece = width // shot_count
    f32 = jnp.float32
    slab = (rows, width, lanes)
    padded = (STEPS, rows + 2 * REACH, width + 2 * PAD, lanes)
    vmem = pl.BlockSpec(memory_space=pltpu.VMEM)
    smem = pl.BlockSpec(memory_space=pltpu.SMEM)
    anywhere = pl.BlockSpec(memory_space=pltpu.HBM)
    dma = pltpu.SemaphoreType.DMA
    return pl.pallas_call(
        functools.partial(kernel, depth_count, shot_count, inner_count),
        out_shape=(
            jax.ShapeDtypeStruct((rows, piece, lanes), f32),
            jax.ShapeDtypeStruct((rows, piece, lanes), f32),
            jax.ShapeDtypeStruct(slab, f32),
        ),
        in_specs=[smem, smem, vmem, vmem] + [anywhere] * 6,
        out_specs=(vmem, vmem, anywhere),
        scratch_shapes=[
            pltpu.VMEM(padded, f32),
            pltpu.VMEM(padded, f32),
            pltpu.VMEM((STEPS,) + slab, f32),
            pltpu.VMEM((STEPS,) + slab, f32),
            pltpu.VMEM(slab, f32),
            pltpu.VMEM(slab, f32),
            pltpu.VMEM(slab, f32),
            pltpu.VMEM(history.shape, f32),
            pltpu.VMEM((STEPS,) + slab, f32),
            pltpu.VMEM((shot_count, rows, piece, lanes), f32),
            pltpu.VMEM((shot_count, rows, piece, lanes), f32),
            pltpu.VMEM((1, lanes), f32),
            pltpu.VMEM((rows, piece, lanes), f32),
            pltpu.VMEM((shot_count, 1, lanes), f32),
            pltpu.VMEM((inner_count, 1, lanes), f32),
            pltpu.VMEM((outer_count, 1, lanes), f32),
            dma((6,)),
            dma((2, STEPS, 2)),
            dma((2, STEPS, 2)),
            dma((3, shot_count)),
            dma((3, shot_count)),
            dma((shot_count,)),
            dma((shot_count,)),
            dma((inner_count,)),
            dma((inner_count,)),
            dma((outer_count,)),
            dma((outer_count,)),
            dma((shot_count,)),
            dma((shot_count,)),
            dma,
        ],
        compiler_params=pltpu.CompilerParams(
            collective_id=0, has_side_effects=True, vmem_limit_bytes=56 * 1024 * 1024
        ),
    )(
        source_cell,
        wavelet,
        receiver_cell,
        residual,
        courant,
        wave_before,
        wave_current,
        adjoint_after,
        adjoint_current,
        history,
    )


def solution(mesh):
    return jax.shard_map(
        per_device,
        mesh=mesh,
        in_specs=(
            P("depth", None, None),
            P("shot", "depth", None, None),
            P("shot", "depth", None, None),
            P("shot", "depth", None, None),
            P("shot", "depth", None, None),
            P("shot"),
            P("shot", None),
            P("shot", None),
            P("shot", None, None),
            P(None, None, "depth", "shot", None),
        ),
        out_specs=(P("depth", "shot", None), P("depth", "shot", None), P("depth", None, None)),
        check_vma=False,
    )
```

```python
import functools

import jax
import jax.numpy as jnp
from jax import lax
from jax.experimental import pallas as pl
from jax.experimental.pallas import tpu as pltpu
from jax.sharding import PartitionSpec as P

STEPS = 4
PAIRS = 5
REACH = 4
BLOCK = 4
PAD = 8
DENOMINATOR = 5040
MESH = pl.DeviceIdType.MESH

coefficients = (-205.0 / 72.0, 8.0 / 5.0, -1.0 / 5.0, 8.0 / 315.0, -1.0 / 560.0)


def in_three(value):
    high = value.astype(jnp.bfloat16)
    rest = value - high.astype(jnp.float32)
    middle = rest.astype(jnp.bfloat16)
    low = (rest - middle.astype(jnp.float32)).astype(jnp.bfloat16)
    return high, middle, low


def kernel(
    depth_count,
    shot_count,
    inner_count,
    source_ref,
    wavelet_hbm,
    receiver_hbm,
    residual_hbm,
    courant_hbm,
    before_hbm,
    current_hbm,
    after_hbm,
    adjoint_hbm,
    history_hbm,
    gradient_out,
    direction_out,
    next_out,
    wavelet_ref,
    receiver_ref,
    residual_ref,
    wave,
    scaled_adj,
    lap,
    adj,
    before,
    after,
    courant,
    history,
    inject,
    terms,
    parts,
    gram,
    next_piece,
    band,
    lateral,
    slots_near,
    slots_outer,
    load_sem,
    halo_send,
    halo_recv,
    part_send,
    part_recv,
    near_send,
    near_recv,
    outer_send,
    outer_recv,
    next_send,
    next_recv,
    next_local,
):
    rows, width, lanes = courant.shape
    here = lax.axis_index("depth")
    me = lax.axis_index("shot")
    outer_count = depth_count // inner_count
    inner_me = lax.rem(here, inner_count)
    outer_me = lax.div(here, inner_count)
    piece = width // shot_count
    first = 0
    last = depth_count - 1

    def shot_peer(step):
        return lax.rem(me + step, shot_count)

    def outer_peer(step):
        return lax.rem(outer_me + step, outer_count)

    def depth_of(outer, inner):
        return outer * inner_count + inner

    barrier = pltpu.get_barrier_semaphore()

    def greet(depth, shot):
        pl.semaphore_signal(barrier, inc=1, device_id=(depth, shot), device_id_type=MESH)

    half = shot_count // 2
    order = [
        (turn, flip, chip, core)
        for turn in range(half)
        for flip in range(2)
        for chip in range(inner_count // 2)
        for core in range(2)
    ]
    order.remove((0, 0, 0, 0))

    def hops(offset):
        turn, flip, chip, core = offset
        return min(turn, half - turn) + (1 if flip else 2 * chip) + 0.1 * core

    order.sort(key=hops, reverse=True)

    def near_peer(offset):
        turn, flip, chip, core = offset
        shot = lax.rem(lax.div(me, 2) + turn, half) * 2 + lax.rem(lax.rem(me, 2) + flip, 2)
        inner = lax.rem(lax.div(inner_me, 2) + chip, inner_count // 2) * 2
        inner = inner + lax.rem(lax.rem(inner_me, 2) + core, 2)
        return depth_of(outer_me, inner), shot

    near_peers = [near_peer(offset) for offset in order]
    turns = sorted(range(1, outer_count), key=lambda turn: -min(turn, outer_count - turn))
    outer_peers = [(depth_of(outer_peer(turn), inner_me), me) for turn in turns]
    for depth, shot in outer_peers + near_peers:
        greet(depth, shot)
    greet(lax.rem(here + 1, depth_count), me)
    greet(lax.rem(here + depth_count - 1, depth_count), me)
    greetings = 2 + len(near_peers) + len(outer_peers)

    inside = pl.ds(REACH, rows)
    across = pl.ds(PAD, width)
    loads = [
        pltpu.make_async_copy(courant_hbm, courant, load_sem.at[0]),
        pltpu.make_async_copy(adjoint_hbm.at[0], adj.at[0], load_sem.at[1]),
        pltpu.make_async_copy(current_hbm.at[0], wave.at[0, inside, across], load_sem.at[2]),
        pltpu.make_async_copy(before_hbm.at[0], before, load_sem.at[3]),
        pltpu.make_async_copy(after_hbm.at[0], after, load_sem.at[4]),
        pltpu.make_async_copy(history_hbm, history, load_sem.at[5]),
        pltpu.make_async_copy(receiver_hbm, receiver_ref, load_sem.at[6]),
        pltpu.make_async_copy(residual_hbm, residual_ref, load_sem.at[7]),
        pltpu.make_async_copy(wavelet_hbm, wavelet_ref, load_sem.at[8]),
    ]
    for load in loads:
        load.start()

    pads = jnp.zeros((rows, PAD, lanes), jnp.float32)
    for field in (wave, scaled_adj):
        for moment in range(STEPS):
            field[moment, pl.ds(REACH, rows), pl.ds(0, PAD), :] = pads
            field[moment, pl.ds(REACH, rows), pl.ds(PAD + width, PAD), :] = pads
    outside = jnp.zeros((REACH, width, lanes), jnp.float32)

    @pl.when(here == first)
    def _():
        for field in (wave, scaled_adj):
            for moment in range(STEPS):
                field[moment, pl.ds(0, REACH), across, :] = outside

    @pl.when(here == last)
    def _():
        for field in (wave, scaled_adj):
            for moment in range(STEPS):
                field[moment, pl.ds(REACH + rows, REACH), across, :] = outside

    def halo_copy(field, number, moment, up, source=None):
        if source is None:
            start = REACH if up else rows
            source = field.at[moment, pl.ds(start, REACH), across]
        target = field.at[moment, pl.ds(REACH + rows if up else 0, REACH), across]
        side = 0 if up else 1
        to = here - 1 if up else here + 1
        return pltpu.make_async_remote_copy(
            src_ref=source,
            dst_ref=target,
            send_sem=halo_send.at[number, moment, side],
            recv_sem=halo_recv.at[number, moment, side],
            device_id=(to, me),
            device_id_type=MESH,
        )

    def send_halo(field, number, moment, up, source=None):
        @pl.when(here > first if up else here < last)
        def _():
            halo_copy(field, number, moment, up, source).start()

    def wait_halo(field, number, moment, above):
        @pl.when(here > first if above else here < last)
        def _():
            halo_copy(field, number, moment, not above).wait_recv()

    pl.semaphore_wait(barrier, greetings)

    send_halo(wave, 0, 0, True, current_hbm.at[0, pl.ds(0, REACH)])
    send_halo(wave, 0, 0, False, current_hbm.at[0, pl.ds(rows - REACH, REACH)])

    loads[0].wait()
    loads[1].wait()

    def first_scaled(z):
        scaled_adj[0, z + REACH, across, :] = courant[z] * adj[0, z]

    def planes(low, high, body):
        def one(z, carry):
            body(z)
            return carry

        lax.fori_loop(low, high, one, 0)

    planes(0, REACH, first_scaled)
    send_halo(scaled_adj, 1, 0, True)
    planes(rows - REACH, rows, first_scaled)
    send_halo(scaled_adj, 1, 0, False)
    planes(REACH, rows - REACH, first_scaled)

    lane_bits = lanes.bit_length() - 1
    for load in loads[6:]:
        load.wait()
    cells = receiver_ref[...]
    count = cells.shape[1]
    cell_rows = lax.shift_right_logical(cells, lane_bits) - here * (rows * width)
    cell_lanes = cells & (lanes - 1)
    lane_hit = lax.broadcasted_iota(jnp.int32, (lanes, count), 0) == cell_lanes
    block = 4 * width
    weights = []
    for moment in range(STEPS):
        value = jnp.where(lane_hit, residual_ref[0, moment : moment + 1, :], 0.0)
        weights.append(in_three(value))

    def inject_block(number, carry):
        ids = lax.broadcasted_iota(jnp.int32, (block, count), 0) + number * block
        hit = jnp.where(ids == cell_rows, 1.0, 0.0).astype(jnp.bfloat16)
        for moment in range(STEPS):
            total = None
            for weight in reversed(weights[moment]):
                product = lax.dot_general(
                    hit, weight, (((1,), (1,)), ((), ())), preferred_element_type=jnp.float32
                )
                total = product if total is None else total + product
            inject[moment, pl.ds(number * 4, 4)] = total.reshape(4, width, lanes)
        return carry

    lax.fori_loop(0, rows // 4, inject_block, 0)

    source = source_ref[0]
    plane_ids = lax.broadcasted_iota(jnp.int32, (width, lanes), 0) * lanes
    plane_ids = plane_ids + lax.broadcasted_iota(jnp.int32, (width, lanes), 1)

    gap = jnp.abs(
        lax.broadcasted_iota(jnp.int32, (lanes, lanes), 0)
        - lax.broadcasted_iota(jnp.int32, (lanes, lanes), 1)
    )
    weight = jnp.zeros((lanes, lanes), jnp.float32)
    for reach in range(1, REACH + 1):
        weight = jnp.where(gap == reach, float(round(DENOMINATOR * coefficients[reach])), weight)
    weight = weight.astype(jnp.bfloat16)
    for number in range(3):
        band[pl.ds(number * lanes, lanes), :] = weight

    def along(field, moment, low, count):
        value = field[moment, pl.ds(low + REACH, count), across, :].reshape(count * width, lanes)
        split = jnp.concatenate(in_three(value), axis=1)
        product = jnp.dot(split, band[...], preferred_element_type=jnp.float32)
        lateral[pl.ds(low, count)] = product.reshape(count, width, lanes)

    def laplace(field, moment, z):
        at = z + REACH
        center = field[moment, at, across, :]
        total = (3.0 * coefficients[0]) * center + (1.0 / DENOMINATOR) * lateral[z]
        for reach in range(1, REACH + 1):
            depth = field[moment, at + reach, across, :] + field[moment, at - reach, across, :]
            side = (
                field[moment, at, pl.ds(PAD + reach, width), :]
                + field[moment, at, pl.ds(PAD - reach, width), :]
            )
            total = total + coefficients[reach] * (depth + side)
        return center, total

    def forward_plane(moment, z):
        center, total = laplace(wave, moment, z)
        lap[moment, z] = total
        if moment < STEPS - 1:
            old = before[z] if moment == 0 else wave[moment - 1, z + REACH, across, :]
            new = 2.0 * center - old + courant[z] * total
            offset = source - (here * rows + z) * (width * lanes)
            new = new + jnp.where(plane_ids == offset, wavelet_ref[0, moment], 0.0)
            wave[moment + 1, z + REACH, across, :] = new

    def adjoint_plane(moment, z):
        _, total = laplace(scaled_adj, moment, z)
        old = after[z] if moment == 0 else adj[moment - 1, z]
        new = 2.0 * adj[moment, z] - old + total + inject[STEPS - 1 - moment, z]
        if moment < STEPS - 1:
            adj[moment + 1, z] = new
            scaled_adj[moment + 1, z + REACH, across, :] = courant[z] * new
        else:
            total = new * lap[0, z]
            for number in range(1, STEPS):
                total = total + adj[number, z] * lap[STEPS - number, z]
            terms[:, z] = total.reshape(shot_count, piece, lanes)

    stretches = ((REACH, rows - 2 * REACH), (0, REACH), (rows - REACH, REACH))

    def part_copy(number, peer, slot):
        start, length = stretches[number]
        return pltpu.make_async_remote_copy(
            src_ref=terms.at[peer, pl.ds(start, length)],
            dst_ref=parts.at[slot, pl.ds(start, length)],
            send_sem=part_send.at[number, peer],
            recv_sem=part_recv.at[number, slot],
            device_id=(here, peer),
            device_id_type=MESH,
        )

    def send_parts(number):
        for step in range(1, shot_count):
            part_copy(number, shot_peer(step), me).start()

    def forward(moment, low, high):
        for start in range(low, high, BLOCK):
            along(wave, moment, start, BLOCK)
        planes(low, high, functools.partial(forward_plane, moment))

    def adjoint(moment, low, high):
        for start in range(low, high, BLOCK):
            along(scaled_adj, moment, start, BLOCK)
        planes(low, high, functools.partial(adjoint_plane, moment))

    loads[2].wait()
    loads[3].wait()
    loads[4].wait()
    for moment in range(STEPS):
        more = moment < STEPS - 1
        forward(moment, REACH, rows - REACH)
        if not more:
            adjoint(moment, REACH, rows - REACH)
            send_parts(0)
        if moment == 0:
            loads[5].wait()
            pairs = [(0, i, j) for j in range(PAIRS) for i in range(j + 1)]
            pairs += [(1, i, j) for j in range(PAIRS) for i in range(j + 1)]

            def gram_plane(z, sums):
                held = [[history[kind, i, z] for i in range(PAIRS)] for kind in range(2)]
                return tuple(
                    total + held[kind][i] * held[1][j]
                    for total, (kind, i, j) in zip(sums, pairs)
                )

            sums = lax.fori_loop(
                0, rows, gram_plane, tuple(jnp.zeros((piece, lanes), jnp.float32) for _ in pairs)
            )
            row_lane = lax.broadcasted_iota(jnp.int32, (1, lanes), 1)
            packed = jnp.zeros((1, lanes), jnp.float32)
            for total, (kind, i, j) in zip(sums, pairs):
                value = jnp.sum(jnp.sum(total, axis=0, keepdims=True), axis=1, keepdims=True)
                spots = [(2 + PAIRS * kind + j) * 8 + i]
                if kind == 1 and i != j:
                    spots.append((2 + PAIRS * kind + i) * 8 + j)
                for spot in spots:
                    packed = jnp.where(row_lane == spot, value, packed)
            gram[...] = packed
        wait_halo(wave, 0, moment, True)
        forward(moment, 0, REACH)
        if more:
            send_halo(wave, 0, moment + 1, True)
        wait_halo(wave, 0, moment, False)
        forward(moment, rows - REACH, rows)
        if more:
            send_halo(wave, 0, moment + 1, False)
        if more:
            adjoint(moment, REACH, rows - REACH)
        wait_halo(scaled_adj, 1, moment, True)
        adjoint(moment, 0, REACH)
        if more:
            send_halo(scaled_adj, 1, moment + 1, True)
        else:
            send_parts(1)
        wait_halo(scaled_adj, 1, moment, False)
        adjoint(moment, rows - REACH, rows)
        if more:
            send_halo(scaled_adj, 1, moment + 1, False)
        else:
            send_parts(2)

    for number in range(len(stretches)):
        for step in range(1, shot_count):
            part_copy(number, me, shot_peer(step)).wait_recv()

    scale = 1.0 / (shot_count * STEPS)

    def own_plane(z, sums):
        total = terms[me, z]
        for step in range(1, shot_count):
            total = total + parts[shot_peer(step), z]
        total = total * scale
        gradient_out[z] = total
        return tuple(
            held + history[number // PAIRS, number % PAIRS, z] * total
            for number, held in enumerate(sums)
        )

    sums = lax.fori_loop(
        0, rows, own_plane, tuple(jnp.zeros((piece, lanes), jnp.float32) for _ in range(2 * PAIRS))
    )
    row_lane = lax.broadcasted_iota(jnp.int32, (1, lanes), 1)
    packed = gram[...]
    for number, total in enumerate(sums):
        value = jnp.sum(jnp.sum(total, axis=0, keepdims=True), axis=1, keepdims=True)
        spot = (number // PAIRS) * 8 + number % PAIRS
        packed = jnp.where(row_lane == spot, value, packed)

    def gather_sum(value, slots, send, recv, mine, peers):
        slots[mine] = value
        for peer in peers:
            pltpu.make_async_remote_copy(
                src_ref=slots.at[mine],
                dst_ref=slots.at[mine],
                send_sem=send,
                recv_sem=recv,
                device_id=peer,
                device_id_type=MESH,
            ).start()
        every = slots.at[pl.ds(0, len(peers))]
        every = pltpu.make_async_remote_copy(
            src_ref=every,
            dst_ref=every,
            send_sem=send,
            recv_sem=recv,
            device_id=peers[0],
            device_id_type=MESH,
        )
        every.wait_recv()
        sums = [slots[slot] for slot in range(len(peers) + 1)]
        while len(sums) > 1:
            sums = [sums[i] + sums[i + 1] for i in range(0, len(sums), 2)]
        every.wait_send()
        return sums[0]

    near_me = me * inner_count + inner_me
    packed = gather_sum(packed, slots_near, near_send, near_recv, near_me, near_peers)
    packed = gather_sum(packed, slots_outer, outer_send, outer_recv, outer_me, outer_peers)

    spread = jnp.broadcast_to(packed, (8, lanes))
    sub = lax.broadcasted_iota(jnp.int32, (8, lanes), 0)
    lane = lax.broadcasted_iota(jnp.int32, (8, lanes), 1)

    def column(spots):
        return jnp.broadcast_to(
            jnp.sum(jnp.where(lane == spots, spread, 0.0), axis=1, keepdims=True), (8, lanes)
        )

    step_grad = column(sub)
    change_grad = column(8 + sub)
    step_change = [column((2 + j) * 8 + sub) for j in range(PAIRS)]
    step_change_row = [column((2 + sub) * 8 + i) for i in range(PAIRS)]
    change_change = [column((2 + PAIRS + j) * 8 + sub) for j in range(PAIRS)]
    curvature = jnp.where(sub < PAIRS, column((2 + sub) * 8 + sub), 1.0)
    inverse = 1.0 / curvature

    def entry(value, i):
        return jnp.broadcast_to(value[i : i + 1, :], (8, lanes))

    alphas = [None] * PAIRS
    running = step_grad
    for i in reversed(range(PAIRS)):
        alphas[i] = entry(inverse * running, i)
        running = running - alphas[i] * step_change[i]
    gamma = entry(curvature, PAIRS - 1) / entry(change_change[PAIRS - 1], PAIRS - 1)
    running = change_grad
    for j in range(PAIRS):
        running = running - alphas[j] * change_change[j]
    running = gamma * running
    gains = []
    for i in range(PAIRS):
        gain = alphas[i] - entry(inverse * running, i)
        gains.append(gain)
        running = running + gain * step_change_row[i]

    own_lateral = pl.ds(pl.multiple_of(me * piece, piece), piece)

    def direction_plane(z, carry):
        search = gradient_out[z]
        for i in range(PAIRS):
            search = search - alphas[i] * history[1, i, z]
        search = gamma * search
        for i in range(PAIRS):
            search = search + gains[i] * history[0, i, z]
        direction_out[z] = -search
        next_piece[z] = courant[z, own_lateral, :] - 0.05 * search
        return carry

    lax.fori_loop(0, rows, direction_plane, 0)

    def next_copy(peer, slot):
        spot = pl.ds(pl.multiple_of(slot * piece, piece), piece)
        return pltpu.make_async_remote_copy(
            src_ref=next_piece,
            dst_ref=next_out.at[:, spot],
            send_sem=next_send.at[peer],
            recv_sem=next_recv.at[slot],
            device_id=(here, peer),
            device_id_type=MESH,
        )

    for step in range(1, shot_count):
        next_copy(shot_peer(step), me).start()
    own = pltpu.make_async_copy(next_piece, next_out.at[:, own_lateral], next_local)
    own.start()

    for number, field in enumerate((wave, scaled_adj)):
        for moment in range(STEPS):
            for up in (True, False):

                @pl.when(here > first if up else here < last)
                def _():
                    halo_copy(field, number, moment, up).wait_send()

    for number in range(len(stretches)):
        for step in range(1, shot_count):
            part_copy(number, shot_peer(step), me).wait_send()
    own.wait()
    for step in range(1, shot_count):
        next_copy(me, shot_peer(step)).wait_recv()
    for step in range(1, shot_count):
        next_copy(shot_peer(step), me).wait_send()


def per_device(
    courant,
    wave_before,
    wave_current,
    adjoint_after,
    adjoint_current,
    source_cell,
    wavelet,
    receiver_cell,
    residual,
    history,
):
    depth_count = lax.axis_size("depth")
    shot_count = lax.axis_size("shot")
    inner_count = 4
    outer_count = depth_count // inner_count
    rows, width, lanes = courant.shape
    piece = width // shot_count
    f32 = jnp.float32
    slab = (rows, width, lanes)
    padded = (STEPS, rows + 2 * REACH, width + 2 * PAD, lanes)
    vmem = pl.BlockSpec(memory_space=pltpu.VMEM)
    anywhere = pl.BlockSpec(memory_space=pltpu.HBM)
    dma = pltpu.SemaphoreType.DMA
    return pl.pallas_call(
        functools.partial(kernel, depth_count, shot_count, inner_count),
        out_shape=(
            jax.ShapeDtypeStruct((rows, piece, lanes), f32),
            jax.ShapeDtypeStruct((rows, piece, lanes), f32),
            jax.ShapeDtypeStruct(slab, f32),
        ),
        in_specs=[pl.BlockSpec(memory_space=pltpu.SMEM)] + [anywhere] * 9,
        out_specs=(vmem, vmem, anywhere),
        scratch_shapes=[
            pltpu.SMEM(wavelet.shape, f32),
            pltpu.VMEM(receiver_cell.shape, jnp.int32),
            pltpu.VMEM(residual.shape, f32),
            pltpu.VMEM(padded, f32),
            pltpu.VMEM(padded, f32),
            pltpu.VMEM((STEPS,) + slab, f32),
            pltpu.VMEM((STEPS,) + slab, f32),
            pltpu.VMEM(slab, f32),
            pltpu.VMEM(slab, f32),
            pltpu.VMEM(slab, f32),
            pltpu.VMEM(history.shape, f32),
            pltpu.VMEM((STEPS,) + slab, f32),
            pltpu.VMEM((shot_count, rows, piece, lanes), f32),
            pltpu.VMEM((shot_count, rows, piece, lanes), f32),
            pltpu.VMEM((1, lanes), f32),
            pltpu.VMEM((rows, piece, lanes), f32),
            pltpu.VMEM((3 * lanes, lanes), jnp.bfloat16),
            pltpu.VMEM(slab, f32),
            pltpu.VMEM((shot_count * inner_count, 1, lanes), f32),
            pltpu.VMEM((outer_count, 1, lanes), f32),
            dma((9,)),
            dma((2, STEPS, 2)),
            dma((2, STEPS, 2)),
            dma((3, shot_count)),
            dma((3, shot_count)),
            dma,
            dma,
            dma,
            dma,
            dma((shot_count,)),
            dma((shot_count,)),
            dma,
        ],
        compiler_params=pltpu.CompilerParams(
            collective_id=0, has_side_effects=True, vmem_limit_bytes=36 * 1024 * 1024
        ),
    )(
        source_cell,
        *(
            pltpu.with_memory_space_constraint(array, pltpu.HBM)
            for array in (
                wavelet,
                receiver_cell,
                residual,
                courant,
                wave_before,
                wave_current,
                adjoint_after,
                adjoint_current,
                history,
            )
        )
    )


def solution(mesh):
    return jax.shard_map(
        per_device,
        mesh=mesh,
        in_specs=(
            P("depth", None, None),
            P("shot", "depth", None, None),
            P("shot", "depth", None, None),
            P("shot", "depth", None, None),
            P("shot", "depth", None, None),
            P("shot"),
            P("shot", None),
            P("shot", None),
            P("shot", None, None),
            P(None, None, "depth", "shot", None),
        ),
        out_specs=(P("depth", "shot", None), P("depth", "shot", None), P("depth", None, None)),
        check_vma=False,
    )
```

```python
import functools

import jax
import jax.numpy as jnp
from jax import lax
from jax.experimental import pallas as pl
from jax.experimental.pallas import tpu as pltpu
from jax.sharding import PartitionSpec as P

STEPS = 4
PAIRS = 5
REACH = 4
BLOCK = 4
PAD = 8
DENOMINATOR = 5040
MESH = pl.DeviceIdType.MESH

coefficients = (-205.0 / 72.0, 8.0 / 5.0, -1.0 / 5.0, 8.0 / 315.0, -1.0 / 560.0)


def in_three(value):
    high = value.astype(jnp.bfloat16)
    rest = value - high.astype(jnp.float32)
    middle = rest.astype(jnp.bfloat16)
    low = (rest - middle.astype(jnp.float32)).astype(jnp.bfloat16)
    return high, middle, low


def kernel(
    depth_count,
    shot_count,
    inner_count,
    source_ref,
    wavelet_hbm,
    receiver_hbm,
    residual_hbm,
    courant_hbm,
    before_hbm,
    current_hbm,
    after_hbm,
    adjoint_hbm,
    history_hbm,
    pair_out,
    next_out,
    wavelet_ref,
    receiver_ref,
    residual_ref,
    wave,
    scaled_adj,
    lap,
    adj,
    before,
    after,
    courant,
    history,
    inject,
    terms,
    parts,
    gram,
    next_piece,
    band,
    lateral,
    slots_near,
    slots_outer,
    load_sem,
    halo_send,
    halo_recv,
    part_send,
    part_recv,
    near_send,
    near_recv,
    outer_send,
    outer_recv,
    next_send,
    next_recv,
    next_local,
):
    rows, width, lanes = courant.shape
    here = lax.axis_index("depth")
    me = lax.axis_index("shot")
    outer_count = depth_count // inner_count
    inner_me = lax.rem(here, inner_count)
    outer_me = lax.div(here, inner_count)
    piece = width // shot_count
    first = 0
    last = depth_count - 1

    def shot_peer(step):
        return lax.rem(me + step, shot_count)

    def outer_peer(step):
        return lax.rem(outer_me + step, outer_count)

    def depth_of(outer, inner):
        return outer * inner_count + inner

    barrier = pltpu.get_barrier_semaphore()

    def greet(depth, shot):
        pl.semaphore_signal(barrier, inc=1, device_id=(depth, shot), device_id_type=MESH)

    half = shot_count // 2
    order = [
        (turn, flip, chip, core)
        for turn in range(half)
        for flip in range(2)
        for chip in range(inner_count // 2)
        for core in range(2)
    ]
    order.remove((0, 0, 0, 0))

    def hops(offset):
        turn, flip, chip, core = offset
        return min(turn, half - turn) + (1 if flip else 2 * chip) + 0.1 * core

    order.sort(key=hops, reverse=True)

    def near_peer(offset):
        turn, flip, chip, core = offset
        shot = lax.rem(lax.div(me, 2) + turn, half) * 2 + lax.rem(lax.rem(me, 2) + flip, 2)
        inner = lax.rem(lax.div(inner_me, 2) + chip, inner_count // 2) * 2
        inner = inner + lax.rem(lax.rem(inner_me, 2) + core, 2)
        return depth_of(outer_me, inner), shot

    near_peers = [near_peer(offset) for offset in order]
    shot_order = sorted(
        range(1, shot_count),
        key=lambda step: (step % 2 == 0, abs(step - half - (step % 2))),
    )
    turns = sorted(range(1, outer_count), key=lambda turn: -min(turn, outer_count - turn))
    outer_peers = [(depth_of(outer_peer(turn), inner_me), me) for turn in turns]
    greet(lax.rem(here + 1, depth_count), me)
    greet(lax.rem(here + depth_count - 1, depth_count), me)
    for depth, shot in outer_peers + near_peers:
        greet(depth, shot)
    greetings = 2 + len(near_peers) + len(outer_peers)

    inside = pl.ds(REACH, rows)
    across = pl.ds(PAD, width)
    loads = [
        pltpu.make_async_copy(courant_hbm, courant, load_sem.at[0]),
        pltpu.make_async_copy(adjoint_hbm.at[0], adj.at[0], load_sem.at[1]),
        pltpu.make_async_copy(current_hbm.at[0], wave.at[0, inside, across], load_sem.at[2]),
        pltpu.make_async_copy(before_hbm.at[0], before, load_sem.at[3]),
        pltpu.make_async_copy(after_hbm.at[0], after, load_sem.at[4]),
        pltpu.make_async_copy(history_hbm, history, load_sem.at[5]),
        pltpu.make_async_copy(receiver_hbm, receiver_ref, load_sem.at[6]),
        pltpu.make_async_copy(residual_hbm, residual_ref, load_sem.at[7]),
        pltpu.make_async_copy(wavelet_hbm, wavelet_ref, load_sem.at[8]),
    ]
    for load in loads:
        load.start()

    upper = lax.rem(here, 2) == 0

    def by_core(if_upper, if_lower):
        return jnp.where(upper, if_upper, if_lower)

    far_low = by_core(0, rows - REACH)
    most_low = by_core(REACH, 0)
    most = rows - REACH
    far_to = by_core(here - 1, here + 1)
    near_to = by_core(here + 1, here - 1)
    has_far = (far_to >= first) & (far_to <= last)

    def halo_copy(field, number, moment, far, source=None):
        if far:
            start, target = by_core(REACH, rows), by_core(REACH + rows, 0)
        else:
            start, target = by_core(rows, REACH), by_core(0, REACH + rows)
        if source is None:
            source = field.at[moment, pl.ds(start, REACH), across]
        else:
            source = source.at[0, pl.ds(start - REACH, REACH)]
        return pltpu.make_async_remote_copy(
            src_ref=source,
            dst_ref=field.at[moment, pl.ds(target, REACH), across],
            send_sem=halo_send.at[number, moment, 1 if far else 0],
            recv_sem=halo_recv.at[number, moment, 1 if far else 0],
            device_id=(far_to if far else near_to, me),
            device_id_type=MESH,
        )

    def when_far(far, body):
        if far:
            pl.when(has_far)(body)
        else:
            body()

    def send_halo(field, number, moment, far, source=None):
        when_far(far, lambda: halo_copy(field, number, moment, far, source).start())

    def wait_halo(field, number, moment, far):
        when_far(far, lambda: halo_copy(field, number, moment, far).wait_recv())

    pl.semaphore_wait(barrier, greetings)

    send_halo(wave, 0, 0, True, current_hbm)
    send_halo(wave, 0, 0, False, current_hbm)

    pads = jnp.zeros((rows, PAD, lanes), jnp.float32)
    for field in (wave, scaled_adj):
        for moment in range(STEPS):
            field[moment, pl.ds(REACH, rows), pl.ds(0, PAD), :] = pads
            field[moment, pl.ds(REACH, rows), pl.ds(PAD + width, PAD), :] = pads
    outside = jnp.zeros((REACH, width, lanes), jnp.float32)

    @pl.when(here == first)
    def _():
        for field in (wave, scaled_adj):
            for moment in range(STEPS):
                field[moment, pl.ds(0, REACH), across, :] = outside

    @pl.when(here == last)
    def _():
        for field in (wave, scaled_adj):
            for moment in range(STEPS):
                field[moment, pl.ds(REACH + rows, REACH), across, :] = outside

    lane_bits = lanes.bit_length() - 1
    for load in loads[6:]:
        load.wait()
    cells = receiver_ref[...]
    count = cells.shape[1]
    cell_rows = lax.shift_right_logical(cells, lane_bits) - here * (rows * width)
    cell_lanes = cells & (lanes - 1)
    lane_hit = lax.broadcasted_iota(jnp.int32, (lanes, count), 0) == cell_lanes
    block = 4 * width
    weights = []
    for moment in range(STEPS):
        value = jnp.where(lane_hit, residual_ref[0, moment : moment + 1, :], 0.0)
        weights.append(in_three(value))

    def inject_block(number, carry):
        ids = lax.broadcasted_iota(jnp.int32, (block, count), 0) + number * block
        hit = jnp.where(ids == cell_rows, 1.0, 0.0).astype(jnp.bfloat16)
        for moment in range(STEPS):
            total = None
            for weight in reversed(weights[moment]):
                product = lax.dot_general(
                    hit, weight, (((1,), (1,)), ((), ())), preferred_element_type=jnp.float32
                )
                total = product if total is None else total + product
            inject[moment, pl.ds(number * 4, 4)] = total.reshape(4, width, lanes)
        return carry

    lax.fori_loop(0, rows // 4, inject_block, 0)

    loads[0].wait()
    loads[1].wait()

    def first_scaled(z):
        scaled_adj[0, z + REACH, across, :] = courant[z] * adj[0, z]

    def planes(low, count, body):
        def one(number, carry):
            for step in range(2):
                body(low + 2 * number + step)
            return carry

        lax.fori_loop(0, count // 2, one, 0)

    planes(far_low, REACH, first_scaled)
    send_halo(scaled_adj, 1, 0, True)
    planes(most_low, most, first_scaled)
    send_halo(scaled_adj, 1, 0, False)

    source = source_ref[0]
    plane_ids = lax.broadcasted_iota(jnp.int32, (width, lanes), 0) * lanes
    plane_ids = plane_ids + lax.broadcasted_iota(jnp.int32, (width, lanes), 1)

    gap = jnp.abs(
        lax.broadcasted_iota(jnp.int32, (lanes, lanes), 0)
        - lax.broadcasted_iota(jnp.int32, (lanes, lanes), 1)
    )
    weight = jnp.zeros((lanes, lanes), jnp.float32)
    for reach in range(1, REACH + 1):
        weight = jnp.where(gap == reach, float(round(DENOMINATOR * coefficients[reach])), weight)
    weight = weight.astype(jnp.bfloat16)
    for number in range(3):
        band[pl.ds(number * lanes, lanes), :] = weight

    def along(field, moment, low, count):
        value = field[moment, pl.ds(low + REACH, count), across, :].reshape(count * width, lanes)
        split = jnp.concatenate(in_three(value), axis=1)
        product = jnp.dot(split, band[...], preferred_element_type=jnp.float32)
        lateral[pl.ds(low, count)] = product.reshape(count, width, lanes)

    def laplace(field, moment, z):
        at = z + REACH
        center = field[moment, at, across, :]
        total = (3.0 * coefficients[0]) * center + (1.0 / DENOMINATOR) * lateral[z]
        for reach in range(1, REACH + 1):
            depth = field[moment, at + reach, across, :] + field[moment, at - reach, across, :]
            side = (
                field[moment, at, pl.ds(PAD + reach, width), :]
                + field[moment, at, pl.ds(PAD - reach, width), :]
            )
            total = total + coefficients[reach] * (depth + side)
        return center, total

    def forward_plane(moment, z):
        center, total = laplace(wave, moment, z)
        lap[moment, z] = total
        if moment < STEPS - 1:
            old = before[z] if moment == 0 else wave[moment - 1, z + REACH, across, :]
            new = 2.0 * center - old + courant[z] * total
            offset = source - (here * rows + z) * (width * lanes)
            new = new + jnp.where(plane_ids == offset, wavelet_ref[0, moment], 0.0)
            wave[moment + 1, z + REACH, across, :] = new

    def adjoint_plane(moment, z):
        _, total = laplace(scaled_adj, moment, z)
        old = after[z] if moment == 0 else adj[moment - 1, z]
        new = 2.0 * adj[moment, z] - old + total + inject[STEPS - 1 - moment, z]
        if moment < STEPS - 1:
            adj[moment + 1, z] = new
            scaled_adj[moment + 1, z + REACH, across, :] = courant[z] * new
        else:
            total = new * lap[0, z]
            for number in range(1, STEPS):
                total = total + adj[number, z] * lap[STEPS - number, z]
            terms[:, z] = total.reshape(shot_count, piece, lanes)

    stretches = ((most_low, most), (far_low, REACH))

    def part_copy(number, peer, slot):
        start, length = stretches[number]
        return pltpu.make_async_remote_copy(
            src_ref=terms.at[peer, pl.ds(start, length)],
            dst_ref=parts.at[slot, pl.ds(start, length)],
            send_sem=part_send.at[number, peer],
            recv_sem=part_recv.at[number, slot],
            device_id=(here, peer),
            device_id_type=MESH,
        )

    def send_parts(number):
        for step in shot_order:
            part_copy(number, shot_peer(step), me).start()

    def forward(moment, low, count):
        for start in range(0, count, BLOCK):
            along(wave, moment, low + start, BLOCK)
        planes(low, count, functools.partial(forward_plane, moment))

    def adjoint(moment, low, count):
        for start in range(0, count, BLOCK):
            along(scaled_adj, moment, low + start, BLOCK)
        planes(low, count, functools.partial(adjoint_plane, moment))

    loads[2].wait()
    loads[3].wait()
    loads[4].wait()
    for moment in range(STEPS):
        more = moment < STEPS - 1
        wait_halo(wave, 0, moment, False)
        forward(moment, most_low, most)
        if more:
            send_halo(wave, 0, moment + 1, False)
        wait_halo(scaled_adj, 1, moment, False)
        adjoint(moment, most_low, most)
        if more:
            send_halo(scaled_adj, 1, moment + 1, False)
        else:
            send_parts(0)
        if moment == 0:
            loads[5].wait()
            pairs = [(0, i, j) for j in range(PAIRS) for i in range(j + 1)]
            pairs += [(1, i, j) for j in range(PAIRS) for i in range(j + 1)]

            def gram_plane(z, sums):
                held = [[history[kind, i, z] for i in range(PAIRS)] for kind in range(2)]
                return tuple(
                    total + held[kind][i] * held[1][j]
                    for total, (kind, i, j) in zip(sums, pairs)
                )

            sums = lax.fori_loop(
                0, rows, gram_plane, tuple(jnp.zeros((piece, lanes), jnp.float32) for _ in pairs)
            )
            row_lane = lax.broadcasted_iota(jnp.int32, (1, lanes), 1)
            packed = jnp.zeros((1, lanes), jnp.float32)
            for total, (kind, i, j) in zip(sums, pairs):
                value = jnp.sum(jnp.sum(total, axis=0, keepdims=True), axis=1, keepdims=True)
                spots = [(2 + PAIRS * kind + j) * 8 + i]
                if kind == 1 and i != j:
                    spots.append((2 + PAIRS * kind + i) * 8 + j)
                for spot in spots:
                    packed = jnp.where(row_lane == spot, value, packed)
            gram[...] = packed
        wait_halo(wave, 0, moment, True)
        forward(moment, far_low, REACH)
        if more:
            send_halo(wave, 0, moment + 1, True)
        wait_halo(scaled_adj, 1, moment, True)
        adjoint(moment, far_low, REACH)
        if more:
            send_halo(scaled_adj, 1, moment + 1, True)
        else:
            send_parts(1)

    for number in range(len(stretches)):
        for step in range(1, shot_count):
            part_copy(number, me, shot_peer(step)).wait_recv()

    scale = 1.0 / (shot_count * STEPS)

    def own_plane(z, sums):
        total = terms[me, z]
        for step in range(1, shot_count):
            total = total + parts[shot_peer(step), z]
        pair_out[0, z] = total
        total = total * scale
        return tuple(
            held + history[number // PAIRS, number % PAIRS, z] * total
            for number, held in enumerate(sums)
        )

    sums = lax.fori_loop(
        0,
        rows,
        own_plane,
        tuple(jnp.zeros((piece, lanes), jnp.float32) for _ in range(2 * PAIRS)),
        unroll=4,
    )
    row_lane = lax.broadcasted_iota(jnp.int32, (1, lanes), 1)
    packed = gram[...]
    for number, total in enumerate(sums):
        value = jnp.sum(jnp.sum(total, axis=0, keepdims=True), axis=1, keepdims=True)
        spot = (number // PAIRS) * 8 + number % PAIRS
        packed = jnp.where(row_lane == spot, value, packed)

    def gather_sum(value, slots, send, recv, mine, peers):
        slots[mine] = value
        for peer in peers:
            pltpu.make_async_remote_copy(
                src_ref=slots.at[mine],
                dst_ref=slots.at[mine],
                send_sem=send,
                recv_sem=recv,
                device_id=peer,
                device_id_type=MESH,
            ).start()
        every = slots.at[pl.ds(0, len(peers))]
        every = pltpu.make_async_remote_copy(
            src_ref=every,
            dst_ref=every,
            send_sem=send,
            recv_sem=recv,
            device_id=peers[0],
            device_id_type=MESH,
        )
        every.wait_recv()
        sums = [slots[slot] for slot in range(len(peers) + 1)]
        while len(sums) > 1:
            sums = [sums[i] + sums[i + 1] for i in range(0, len(sums), 2)]
        every.wait_send()
        return sums[0]

    near_me = me * inner_count + inner_me
    packed = gather_sum(packed, slots_near, near_send, near_recv, near_me, near_peers)
    packed = gather_sum(packed, slots_outer, outer_send, outer_recv, outer_me, outer_peers)

    spread = jnp.broadcast_to(packed, (8, lanes))
    sub = lax.broadcasted_iota(jnp.int32, (8, lanes), 0)
    lane = lax.broadcasted_iota(jnp.int32, (8, lanes), 1)

    def column(spots):
        return jnp.broadcast_to(
            jnp.sum(jnp.where(lane == spots, spread, 0.0), axis=1, keepdims=True), (8, lanes)
        )

    step_grad = column(sub)
    change_grad = column(8 + sub)
    step_change = [column((2 + j) * 8 + sub) for j in range(PAIRS)]
    step_change_row = [column((2 + sub) * 8 + i) for i in range(PAIRS)]
    change_change = [column((2 + PAIRS + j) * 8 + sub) for j in range(PAIRS)]
    curvature = jnp.where(sub < PAIRS, column((2 + sub) * 8 + sub), 1.0)
    inverse = 1.0 / curvature

    def entry(value, i):
        return jnp.broadcast_to(value[i : i + 1, :], (8, lanes))

    alphas = [None] * PAIRS
    running = step_grad
    for i in reversed(range(PAIRS)):
        alphas[i] = entry(inverse * running, i)
        running = running - alphas[i] * step_change[i]
    gamma = entry(curvature, PAIRS - 1) / entry(change_change[PAIRS - 1], PAIRS - 1)
    running = change_grad
    for j in range(PAIRS):
        running = running - alphas[j] * change_change[j]
    running = gamma * running
    gains = []
    for i in range(PAIRS):
        gain = alphas[i] - entry(inverse * running, i)
        gains.append(gain)
        running = running + gain * step_change_row[i]

    own_lateral = pl.ds(pl.multiple_of(me * piece, piece), piece)

    def direction_plane(z, carry):
        search = pair_out[0, z] * scale
        for i in range(PAIRS):
            search = search - alphas[i] * history[1, i, z]
        search = gamma * search
        for i in range(PAIRS):
            search = search + gains[i] * history[0, i, z]
        pair_out[1, z] = search
        next_piece[z] = courant[z, own_lateral, :] - 0.05 * search
        return carry

    lax.fori_loop(0, rows, direction_plane, 0, unroll=4)

    def next_copy(peer, slot):
        spot = pl.ds(pl.multiple_of(slot * piece, piece), piece)
        return pltpu.make_async_remote_copy(
            src_ref=next_piece,
            dst_ref=next_out.at[:, spot],
            send_sem=next_send.at[peer],
            recv_sem=next_recv.at[slot],
            device_id=(here, peer),
            device_id_type=MESH,
        )

    for step in shot_order:
        next_copy(shot_peer(step), me).start()
    own = pltpu.make_async_copy(next_piece, next_out.at[:, own_lateral], next_local)
    own.start()

    for number, field in enumerate((wave, scaled_adj)):
        for moment in range(STEPS):
            when_far(True, halo_copy(field, number, moment, True).wait_send)
            halo_copy(field, number, moment, False).wait_send()

    for number in range(len(stretches)):
        for step in range(1, shot_count):
            part_copy(number, shot_peer(step), me).wait_send()
    own.wait()
    for step in range(1, shot_count):
        next_copy(me, shot_peer(step)).wait_recv()
    for step in range(1, shot_count):
        next_copy(shot_peer(step), me).wait_send()


def per_device(
    courant,
    wave_before,
    wave_current,
    adjoint_after,
    adjoint_current,
    source_cell,
    wavelet,
    receiver_cell,
    residual,
    history,
):
    depth_count = lax.axis_size("depth")
    shot_count = lax.axis_size("shot")
    inner_count = 4
    outer_count = depth_count // inner_count
    rows, width, lanes = courant.shape
    piece = width // shot_count
    f32 = jnp.float32
    slab = (rows, width, lanes)
    padded = (STEPS, rows + 2 * REACH, width + 2 * PAD, lanes)
    vmem = pl.BlockSpec(memory_space=pltpu.VMEM)
    anywhere = pl.BlockSpec(memory_space=pltpu.HBM)
    dma = pltpu.SemaphoreType.DMA
    pair, courant_next = pl.pallas_call(
        functools.partial(kernel, depth_count, shot_count, inner_count),
        out_shape=(
            jax.ShapeDtypeStruct((2, rows, piece, lanes), f32),
            jax.ShapeDtypeStruct(slab, f32),
        ),
        in_specs=[pl.BlockSpec(memory_space=pltpu.SMEM)] + [anywhere] * 9,
        out_specs=(vmem, anywhere),
        scratch_shapes=[
            pltpu.SMEM(wavelet.shape, f32),
            pltpu.VMEM(receiver_cell.shape, jnp.int32),
            pltpu.VMEM(residual.shape, f32),
            pltpu.VMEM(padded, f32),
            pltpu.VMEM(padded, f32),
            pltpu.VMEM((STEPS,) + slab, f32),
            pltpu.VMEM((STEPS,) + slab, f32),
            pltpu.VMEM(slab, f32),
            pltpu.VMEM(slab, f32),
            pltpu.VMEM(slab, f32),
            pltpu.VMEM(history.shape, f32),
            pltpu.VMEM((STEPS,) + slab, f32),
            pltpu.VMEM((shot_count, rows, piece, lanes), f32),
            pltpu.VMEM((shot_count, rows, piece, lanes), f32),
            pltpu.VMEM((1, lanes), f32),
            pltpu.VMEM((rows, piece, lanes), f32),
            pltpu.VMEM((3 * lanes, lanes), jnp.bfloat16),
            pltpu.VMEM(slab, f32),
            pltpu.VMEM((shot_count * inner_count, 1, lanes), f32),
            pltpu.VMEM((outer_count, 1, lanes), f32),
            dma((9,)),
            dma((2, STEPS, 2)),
            dma((2, STEPS, 2)),
            dma((2, shot_count)),
            dma((2, shot_count)),
            dma,
            dma,
            dma,
            dma,
            dma((shot_count,)),
            dma((shot_count,)),
            dma,
        ],
        compiler_params=pltpu.CompilerParams(
            collective_id=0, has_side_effects=True, vmem_limit_bytes=36 * 1024 * 1024
        ),
    )(
        source_cell,
        *(
            pltpu.with_memory_space_constraint(array, pltpu.HBM)
            for array in (
                wavelet,
                receiver_cell,
                residual,
                courant,
                wave_before,
                wave_current,
                adjoint_after,
                adjoint_current,
                history,
            )
        )
    )
    return pair[0] * (1.0 / (shot_count * STEPS)), -pair[1], courant_next


def solution(mesh):
    return jax.shard_map(
        per_device,
        mesh=mesh,
        in_specs=(
            P("depth", None, None),
            P("shot", "depth", None, None),
            P("shot", "depth", None, None),
            P("shot", "depth", None, None),
            P("shot", "depth", None, None),
            P("shot"),
            P("shot", None),
            P("shot", None),
            P("shot", None, None),
            P(None, None, "depth", "shot", None),
        ),
        out_specs=(P("depth", "shot", None), P("depth", "shot", None), P("depth", None, None)),
        check_vma=False,
    )
```

```python
import functools

import jax
import jax.numpy as jnp
from jax import lax
from jax.experimental import pallas as pl
from jax.experimental.pallas import tpu as pltpu
from jax.sharding import PartitionSpec as P

STEPS = 4
PAIRS = 5
REACH = 4
BLOCK = 4
PAD = 8
DENOMINATOR = 5040
MESH = pl.DeviceIdType.MESH

coefficients = (-205.0 / 72.0, 8.0 / 5.0, -1.0 / 5.0, 8.0 / 315.0, -1.0 / 560.0)


def in_three(value):
    high = value.astype(jnp.bfloat16)
    rest = value - high.astype(jnp.float32)
    middle = rest.astype(jnp.bfloat16)
    low = (rest - middle.astype(jnp.float32)).astype(jnp.bfloat16)
    return high, middle, low


def kernel(
    depth_count,
    shot_count,
    inner_count,
    source_ref,
    wavelet_hbm,
    receiver_hbm,
    residual_hbm,
    courant_hbm,
    before_hbm,
    current_hbm,
    after_hbm,
    adjoint_hbm,
    history_hbm,
    pair_out,
    next_out,
    wavelet_ref,
    receiver_ref,
    residual_ref,
    wave,
    scaled_adj,
    lap,
    adj,
    before,
    after,
    courant,
    history,
    inject,
    terms,
    parts,
    gram,
    next_piece,
    band,
    lateral,
    slots_near,
    slots_outer,
    load_sem,
    halo_send,
    halo_recv,
    part_send,
    part_recv,
    near_send,
    near_recv,
    outer_send,
    outer_recv,
    next_send,
    next_recv,
    next_local,
):
    rows, width, lanes = courant.shape
    here = lax.axis_index("depth")
    me = lax.axis_index("shot")
    outer_count = depth_count // inner_count
    inner_me = lax.rem(here, inner_count)
    outer_me = lax.div(here, inner_count)
    piece = width // shot_count
    first = 0
    last = depth_count - 1

    def shot_peer(step):
        return lax.rem(me + step, shot_count)

    def outer_peer(step):
        return lax.rem(outer_me + step, outer_count)

    def depth_of(outer, inner):
        return outer * inner_count + inner

    barrier = pltpu.get_barrier_semaphore()

    def greet(depth, shot):
        pl.semaphore_signal(barrier, inc=1, device_id=(depth, shot), device_id_type=MESH)

    half = shot_count // 2
    order = [
        (turn, flip, chip, core)
        for turn in range(half)
        for flip in range(2)
        for chip in range(inner_count // 2)
        for core in range(2)
    ]
    order.remove((0, 0, 0, 0))

    def hops(offset):
        turn, flip, chip, core = offset
        return min(turn, half - turn) + (1 if flip else 2 * chip) + 0.1 * core

    order.sort(key=hops, reverse=True)

    def near_peer(offset):
        turn, flip, chip, core = offset
        shot = lax.rem(lax.div(me, 2) + turn, half) * 2 + lax.rem(lax.rem(me, 2) + flip, 2)
        inner = lax.rem(lax.div(inner_me, 2) + chip, inner_count // 2) * 2
        inner = inner + lax.rem(lax.rem(inner_me, 2) + core, 2)
        return depth_of(outer_me, inner), shot

    near_peers = [near_peer(offset) for offset in order]
    shot_order = sorted(
        range(1, shot_count),
        key=lambda step: (step % 2 == 0, abs(step - half - (step % 2))),
    )
    turns = sorted(range(1, outer_count), key=lambda turn: -min(turn, outer_count - turn))
    outer_peers = [(depth_of(outer_peer(turn), inner_me), me) for turn in turns]
    greet(lax.rem(here + 1, depth_count), me)
    greet(lax.rem(here + depth_count - 1, depth_count), me)
    for depth, shot in outer_peers + near_peers:
        greet(depth, shot)
    greetings = 2 + len(near_peers) + len(outer_peers)

    inside = pl.ds(REACH, rows)
    across = pl.ds(PAD, width)
    loads = [
        pltpu.make_async_copy(courant_hbm, courant, load_sem.at[0]),
        pltpu.make_async_copy(adjoint_hbm.at[0], adj.at[0], load_sem.at[1]),
        pltpu.make_async_copy(current_hbm.at[0], wave.at[0, inside, across], load_sem.at[2]),
        pltpu.make_async_copy(before_hbm.at[0], before, load_sem.at[3]),
        pltpu.make_async_copy(after_hbm.at[0], after, load_sem.at[4]),
        pltpu.make_async_copy(history_hbm, history, load_sem.at[5]),
        pltpu.make_async_copy(receiver_hbm, receiver_ref, load_sem.at[6]),
        pltpu.make_async_copy(residual_hbm, residual_ref, load_sem.at[7]),
        pltpu.make_async_copy(wavelet_hbm, wavelet_ref, load_sem.at[8]),
    ]
    for load in loads:
        load.start()

    upper = lax.rem(here, 2) == 0

    def by_core(if_upper, if_lower):
        return jnp.where(upper, if_upper, if_lower)

    far_low = by_core(0, rows - REACH)
    most_low = by_core(REACH, 0)
    most = rows - REACH
    far_to = by_core(here - 1, here + 1)
    near_to = by_core(here + 1, here - 1)
    has_far = (far_to >= first) & (far_to <= last)

    def halo_copy(field, number, moment, far, source=None):
        if far:
            start, target = by_core(REACH, rows), by_core(REACH + rows, 0)
        else:
            start, target = by_core(rows, REACH), by_core(0, REACH + rows)
        if source is None:
            source = field.at[moment, pl.ds(start, REACH), across]
        else:
            source = source.at[0, pl.ds(start - REACH, REACH)]
        return pltpu.make_async_remote_copy(
            src_ref=source,
            dst_ref=field.at[moment, pl.ds(target, REACH), across],
            send_sem=halo_send.at[number, moment, 1 if far else 0],
            recv_sem=halo_recv.at[number, moment, 1 if far else 0],
            device_id=(far_to if far else near_to, me),
            device_id_type=MESH,
        )

    def when_far(far, body):
        if far:
            pl.when(has_far)(body)
        else:
            body()

    def send_halo(field, number, moment, far, source=None):
        when_far(far, lambda: halo_copy(field, number, moment, far, source).start())

    def wait_halo(field, number, moment, far):
        when_far(far, lambda: halo_copy(field, number, moment, far).wait_recv())

    pl.semaphore_wait(barrier, greetings)

    send_halo(wave, 0, 0, True, current_hbm)
    send_halo(wave, 0, 0, False, current_hbm)

    pads = jnp.zeros((rows, PAD, lanes), jnp.float32)
    for field in (wave, scaled_adj):
        for moment in range(STEPS):
            field[moment, pl.ds(REACH, rows), pl.ds(0, PAD), :] = pads
            field[moment, pl.ds(REACH, rows), pl.ds(PAD + width, PAD), :] = pads
    outside = jnp.zeros((REACH, width, lanes), jnp.float32)

    @pl.when(here == first)
    def _():
        for field in (wave, scaled_adj):
            for moment in range(STEPS):
                field[moment, pl.ds(0, REACH), across, :] = outside

    @pl.when(here == last)
    def _():
        for field in (wave, scaled_adj):
            for moment in range(STEPS):
                field[moment, pl.ds(REACH + rows, REACH), across, :] = outside

    lane_bits = lanes.bit_length() - 1
    for load in loads[6:]:
        load.wait()
    cells = receiver_ref[...]
    count = cells.shape[1]
    cell_rows = lax.shift_right_logical(cells, lane_bits) - here * (rows * width)
    cell_lanes = cells & (lanes - 1)
    lane_hit = lax.broadcasted_iota(jnp.int32, (lanes, count), 0) == cell_lanes
    block = 4 * width
    weights = []
    for moment in range(STEPS):
        value = jnp.where(lane_hit, residual_ref[0, moment : moment + 1, :], 0.0)
        weights.append(in_three(value))

    def inject_block(number, carry):
        ids = lax.broadcasted_iota(jnp.int32, (block, count), 0) + number * block
        hit = jnp.where(ids == cell_rows, 1.0, 0.0).astype(jnp.bfloat16)
        for moment in range(STEPS):
            total = None
            for weight in reversed(weights[moment]):
                product = lax.dot_general(
                    hit, weight, (((1,), (1,)), ((), ())), preferred_element_type=jnp.float32
                )
                total = product if total is None else total + product
            inject[moment, pl.ds(number * 4, 4)] = total.reshape(4, width, lanes)
        return carry

    lax.fori_loop(0, rows // 4, inject_block, 0)

    loads[0].wait()
    loads[1].wait()

    def first_scaled(z):
        scaled_adj[0, z + REACH, across, :] = courant[z] * adj[0, z]

    def planes(low, count, body):
        def one(number, carry):
            for step in range(2):
                body(low + 2 * number + step)
            return carry

        lax.fori_loop(0, count // 2, one, 0)

    planes(far_low, REACH, first_scaled)
    send_halo(scaled_adj, 1, 0, True)
    planes(most_low, most, first_scaled)
    send_halo(scaled_adj, 1, 0, False)

    source = source_ref[0]
    plane_ids = lax.broadcasted_iota(jnp.int32, (width, lanes), 0) * lanes
    plane_ids = plane_ids + lax.broadcasted_iota(jnp.int32, (width, lanes), 1)

    gap = jnp.abs(
        lax.broadcasted_iota(jnp.int32, (lanes, lanes), 0)
        - lax.broadcasted_iota(jnp.int32, (lanes, lanes), 1)
    )
    weight = jnp.zeros((lanes, lanes), jnp.float32)
    for reach in range(1, REACH + 1):
        weight = jnp.where(gap == reach, float(round(DENOMINATOR * coefficients[reach])), weight)
    weight = weight.astype(jnp.bfloat16)
    for number in range(3):
        band[pl.ds(number * lanes, lanes), :] = weight

    def along(field, moment, low, count):
        value = field[moment, pl.ds(low + REACH, count), across, :].reshape(count * width, lanes)
        split = jnp.concatenate(in_three(value), axis=1)
        product = jnp.dot(split, band[...], preferred_element_type=jnp.float32)
        lateral[pl.ds(low, count)] = product.reshape(count, width, lanes)

    def laplace(field, moment, z):
        at = z + REACH
        center = field[moment, at, across, :]
        total = (3.0 * coefficients[0]) * center + (1.0 / DENOMINATOR) * lateral[z]
        for reach in range(1, REACH + 1):
            depth = field[moment, at + reach, across, :] + field[moment, at - reach, across, :]
            side = (
                field[moment, at, pl.ds(PAD + reach, width), :]
                + field[moment, at, pl.ds(PAD - reach, width), :]
            )
            total = total + coefficients[reach] * (depth + side)
        return center, total

    def forward_plane(moment, z):
        center, total = laplace(wave, moment, z)
        lap[moment, z] = total
        if moment < STEPS - 1:
            old = before[z] if moment == 0 else wave[moment - 1, z + REACH, across, :]
            new = 2.0 * center - old + courant[z] * total
            offset = source - (here * rows + z) * (width * lanes)
            new = new + jnp.where(plane_ids == offset, wavelet_ref[0, moment], 0.0)
            wave[moment + 1, z + REACH, across, :] = new

    def adjoint_plane(moment, z):
        _, total = laplace(scaled_adj, moment, z)
        old = after[z] if moment == 0 else adj[moment - 1, z]
        new = 2.0 * adj[moment, z] - old + total + inject[STEPS - 1 - moment, z]
        if moment < STEPS - 1:
            adj[moment + 1, z] = new
            scaled_adj[moment + 1, z + REACH, across, :] = courant[z] * new
        else:
            total = new * lap[0, z]
            for number in range(1, STEPS):
                total = total + adj[number, z] * lap[STEPS - number, z]
            terms[:, z] = total.reshape(shot_count, piece, lanes)

    stretches = ((most_low, most), (far_low, REACH))

    def part_copy(number, peer, slot):
        start, length = stretches[number]
        return pltpu.make_async_remote_copy(
            src_ref=terms.at[peer, pl.ds(start, length)],
            dst_ref=parts.at[slot, pl.ds(start, length)],
            send_sem=part_send.at[number, peer],
            recv_sem=part_recv.at[number, slot],
            device_id=(here, peer),
            device_id_type=MESH,
        )

    def send_parts(number):
        for step in shot_order:
            part_copy(number, shot_peer(step), me).start()

    def forward(moment, low, count):
        for start in range(0, count, BLOCK):
            along(wave, moment, low + start, BLOCK)
        planes(low, count, functools.partial(forward_plane, moment))

    def adjoint(moment, low, count):
        for start in range(0, count, BLOCK):
            along(scaled_adj, moment, low + start, BLOCK)
        planes(low, count, functools.partial(adjoint_plane, moment))

    loads[2].wait()
    loads[3].wait()
    loads[4].wait()
    for moment in range(STEPS):
        more = moment < STEPS - 1
        wait_halo(wave, 0, moment, False)
        forward(moment, most_low, most)
        if more:
            send_halo(wave, 0, moment + 1, False)
        wait_halo(scaled_adj, 1, moment, False)
        adjoint(moment, most_low, most)
        if more:
            send_halo(scaled_adj, 1, moment + 1, False)
        else:
            send_parts(0)
        wait_halo(wave, 0, moment, True)
        forward(moment, far_low, REACH)
        if more:
            send_halo(wave, 0, moment + 1, True)
        wait_halo(scaled_adj, 1, moment, True)
        adjoint(moment, far_low, REACH)
        if more:
            send_halo(scaled_adj, 1, moment + 1, True)
        else:
            send_parts(1)

    loads[5].wait()
    pairs = [(0, i, j) for j in range(PAIRS) for i in range(j + 1)]
    pairs += [(1, i, j) for j in range(PAIRS) for i in range(j + 1)]

    def gram_plane(z, sums):
        held = [[history[kind, i, z] for i in range(PAIRS)] for kind in range(2)]
        return tuple(
            total + held[kind][i] * held[1][j]
            for total, (kind, i, j) in zip(sums, pairs)
        )

    sums = lax.fori_loop(
        0, rows, gram_plane, tuple(jnp.zeros((piece, lanes), jnp.float32) for _ in pairs)
    )
    row_lane = lax.broadcasted_iota(jnp.int32, (1, lanes), 1)
    packed = jnp.zeros((1, lanes), jnp.float32)
    for total, (kind, i, j) in zip(sums, pairs):
        value = jnp.sum(jnp.sum(total, axis=0, keepdims=True), axis=1, keepdims=True)
        spots = [(2 + PAIRS * kind + j) * 8 + i]
        if kind == 1 and i != j:
            spots.append((2 + PAIRS * kind + i) * 8 + j)
        for spot in spots:
            packed = jnp.where(row_lane == spot, value, packed)
    gram[...] = packed

    for number in range(len(stretches)):
        for step in range(1, shot_count):
            part_copy(number, me, shot_peer(step)).wait_recv()

    scale = 1.0 / (shot_count * STEPS)

    def own_plane(z, sums):
        total = terms[me, z]
        for step in range(1, shot_count):
            total = total + parts[shot_peer(step), z]
        pair_out[0, z] = total
        total = total * scale
        return tuple(
            held + history[number // PAIRS, number % PAIRS, z] * total
            for number, held in enumerate(sums)
        )

    sums = lax.fori_loop(
        0,
        rows,
        own_plane,
        tuple(jnp.zeros((piece, lanes), jnp.float32) for _ in range(2 * PAIRS)),
        unroll=4,
    )
    row_lane = lax.broadcasted_iota(jnp.int32, (1, lanes), 1)
    packed = gram[...]
    for number, total in enumerate(sums):
        value = jnp.sum(jnp.sum(total, axis=0, keepdims=True), axis=1, keepdims=True)
        spot = (number // PAIRS) * 8 + number % PAIRS
        packed = jnp.where(row_lane == spot, value, packed)

    def gather_sum(value, slots, send, recv, mine, peers):
        slots[mine] = value
        for peer in peers:
            pltpu.make_async_remote_copy(
                src_ref=slots.at[mine],
                dst_ref=slots.at[mine],
                send_sem=send,
                recv_sem=recv,
                device_id=peer,
                device_id_type=MESH,
            ).start()
        every = slots.at[pl.ds(0, len(peers))]
        every = pltpu.make_async_remote_copy(
            src_ref=every,
            dst_ref=every,
            send_sem=send,
            recv_sem=recv,
            device_id=peers[0],
            device_id_type=MESH,
        )
        every.wait_recv()
        sums = [slots[slot] for slot in range(len(peers) + 1)]
        while len(sums) > 1:
            sums = [sums[i] + sums[i + 1] for i in range(0, len(sums), 2)]
        return sums[0], every

    near_me = me * inner_count + inner_me
    packed, near_every = gather_sum(packed, slots_near, near_send, near_recv, near_me, near_peers)
    packed, outer_every = gather_sum(packed, slots_outer, outer_send, outer_recv, outer_me, outer_peers)

    spread = jnp.broadcast_to(packed, (8, lanes))
    sub = lax.broadcasted_iota(jnp.int32, (8, lanes), 0)
    lane = lax.broadcasted_iota(jnp.int32, (8, lanes), 1)

    def column(spots):
        return jnp.broadcast_to(
            jnp.sum(jnp.where(lane == spots, spread, 0.0), axis=1, keepdims=True), (8, lanes)
        )

    step_grad = column(sub)
    change_grad = column(8 + sub)
    step_change = [column((2 + j) * 8 + sub) for j in range(PAIRS)]
    step_change_row = [column((2 + sub) * 8 + i) for i in range(PAIRS)]
    change_change = [column((2 + PAIRS + j) * 8 + sub) for j in range(PAIRS)]
    curvature = jnp.where(sub < PAIRS, column((2 + sub) * 8 + sub), 1.0)
    inverse = 1.0 / curvature

    def entry(value, i):
        return jnp.broadcast_to(value[i : i + 1, :], (8, lanes))

    alphas = [None] * PAIRS
    running = step_grad
    for i in reversed(range(PAIRS)):
        alphas[i] = entry(inverse * running, i)
        running = running - alphas[i] * step_change[i]
    gamma = entry(curvature, PAIRS - 1) / entry(change_change[PAIRS - 1], PAIRS - 1)
    running = change_grad
    for j in range(PAIRS):
        running = running - alphas[j] * change_change[j]
    running = gamma * running
    gains = []
    for i in range(PAIRS):
        gain = alphas[i] - entry(inverse * running, i)
        gains.append(gain)
        running = running + gain * step_change_row[i]

    own_lateral = pl.ds(pl.multiple_of(me * piece, piece), piece)

    def direction_plane(z, carry):
        search = pair_out[0, z] * scale
        for i in range(PAIRS):
            search = search - alphas[i] * history[1, i, z]
        search = gamma * search
        for i in range(PAIRS):
            search = search + gains[i] * history[0, i, z]
        pair_out[1, z] = search
        next_piece[z] = courant[z, own_lateral, :] - 0.05 * search
        return carry

    lax.fori_loop(0, rows, direction_plane, 0, unroll=4)

    def next_copy(peer, slot):
        spot = pl.ds(pl.multiple_of(slot * piece, piece), piece)
        return pltpu.make_async_remote_copy(
            src_ref=next_piece,
            dst_ref=next_out.at[:, spot],
            send_sem=next_send.at[peer],
            recv_sem=next_recv.at[slot],
            device_id=(here, peer),
            device_id_type=MESH,
        )

    for step in shot_order:
        next_copy(shot_peer(step), me).start()
    own = pltpu.make_async_copy(next_piece, next_out.at[:, own_lateral], next_local)
    own.start()

    for number, field in enumerate((wave, scaled_adj)):
        for moment in range(STEPS):
            when_far(True, halo_copy(field, number, moment, True).wait_send)
            halo_copy(field, number, moment, False).wait_send()

    for number in range(len(stretches)):
        for step in range(1, shot_count):
            part_copy(number, shot_peer(step), me).wait_send()
    near_every.wait_send()
    outer_every.wait_send()
    own.wait()
    for step in range(1, shot_count):
        next_copy(me, shot_peer(step)).wait_recv()
    for step in range(1, shot_count):
        next_copy(shot_peer(step), me).wait_send()


def per_device(
    courant,
    wave_before,
    wave_current,
    adjoint_after,
    adjoint_current,
    source_cell,
    wavelet,
    receiver_cell,
    residual,
    history,
):
    depth_count = lax.axis_size("depth")
    shot_count = lax.axis_size("shot")
    inner_count = 4
    outer_count = depth_count // inner_count
    rows, width, lanes = courant.shape
    piece = width // shot_count
    f32 = jnp.float32
    slab = (rows, width, lanes)
    padded = (STEPS, rows + 2 * REACH, width + 2 * PAD, lanes)
    vmem = pl.BlockSpec(memory_space=pltpu.VMEM)
    anywhere = pl.BlockSpec(memory_space=pltpu.HBM)
    dma = pltpu.SemaphoreType.DMA
    pair, courant_next = pl.pallas_call(
        functools.partial(kernel, depth_count, shot_count, inner_count),
        out_shape=(
            jax.ShapeDtypeStruct((2, rows, piece, lanes), f32),
            jax.ShapeDtypeStruct(slab, f32),
        ),
        in_specs=[pl.BlockSpec(memory_space=pltpu.SMEM)] + [anywhere] * 9,
        out_specs=(vmem, anywhere),
        scratch_shapes=[
            pltpu.SMEM(wavelet.shape, f32),
            pltpu.VMEM(receiver_cell.shape, jnp.int32),
            pltpu.VMEM(residual.shape, f32),
            pltpu.VMEM(padded, f32),
            pltpu.VMEM(padded, f32),
            pltpu.VMEM((STEPS,) + slab, f32),
            pltpu.VMEM((STEPS,) + slab, f32),
            pltpu.VMEM(slab, f32),
            pltpu.VMEM(slab, f32),
            pltpu.VMEM(slab, f32),
            pltpu.VMEM(history.shape, f32),
            pltpu.VMEM((STEPS,) + slab, f32),
            pltpu.VMEM((shot_count, rows, piece, lanes), f32),
            pltpu.VMEM((shot_count, rows, piece, lanes), f32),
            pltpu.VMEM((1, lanes), f32),
            pltpu.VMEM((rows, piece, lanes), f32),
            pltpu.VMEM((3 * lanes, lanes), jnp.bfloat16),
            pltpu.VMEM(slab, f32),
            pltpu.VMEM((shot_count * inner_count, 1, lanes), f32),
            pltpu.VMEM((outer_count, 1, lanes), f32),
            dma((9,)),
            dma((2, STEPS, 2)),
            dma((2, STEPS, 2)),
            dma((2, shot_count)),
            dma((2, shot_count)),
            dma,
            dma,
            dma,
            dma,
            dma((shot_count,)),
            dma((shot_count,)),
            dma,
        ],
        compiler_params=pltpu.CompilerParams(
            collective_id=0, has_side_effects=True, vmem_limit_bytes=36 * 1024 * 1024
        ),
    )(
        source_cell,
        *(
            pltpu.with_memory_space_constraint(array, pltpu.HBM)
            for array in (
                wavelet,
                receiver_cell,
                residual,
                courant,
                wave_before,
                wave_current,
                adjoint_after,
                adjoint_current,
                history,
            )
        )
    )
    return pair[0] * (1.0 / (shot_count * STEPS)), -pair[1], courant_next


def solution(mesh):
    return jax.shard_map(
        per_device,
        mesh=mesh,
        in_specs=(
            P("depth", None, None),
            P("shot", "depth", None, None),
            P("shot", "depth", None, None),
            P("shot", "depth", None, None),
            P("shot", "depth", None, None),
            P("shot"),
            P("shot", None),
            P("shot", None),
            P("shot", None, None),
            P(None, None, "depth", "shot", None),
        ),
        out_specs=(P("depth", "shot", None), P("depth", "shot", None), P("depth", None, None)),
        check_vma=False,
    )
```

```python
import functools

import jax
import jax.numpy as jnp
from jax import lax
from jax.experimental import pallas as pl
from jax.experimental.pallas import tpu as pltpu
from jax.sharding import PartitionSpec as P

STEPS = 4
PAIRS = 5
REACH = 4
BLOCK = 4
PAD = 8
DENOMINATOR = 5040
MESH = pl.DeviceIdType.MESH

coefficients = (-205.0 / 72.0, 8.0 / 5.0, -1.0 / 5.0, 8.0 / 315.0, -1.0 / 560.0)


def in_three(value):
    high = value.astype(jnp.bfloat16)
    rest = value - high.astype(jnp.float32)
    middle = rest.astype(jnp.bfloat16)
    low = (rest - middle.astype(jnp.float32)).astype(jnp.bfloat16)
    return high, middle, low


def kernel(
    depth_count,
    shot_count,
    inner_count,
    source_ref,
    wavelet_hbm,
    receiver_hbm,
    residual_hbm,
    courant_hbm,
    before_hbm,
    current_hbm,
    after_hbm,
    adjoint_hbm,
    history_hbm,
    pair_out,
    next_out,
    wavelet_ref,
    receiver_ref,
    residual_ref,
    wave,
    scaled_adj,
    lap,
    adj,
    before,
    after,
    courant,
    history,
    inject,
    terms,
    parts,
    gram,
    next_piece,
    band,
    lateral,
    slots_near,
    slots_outer,
    load_sem,
    halo_send,
    halo_recv,
    part_send,
    part_recv,
    near_send,
    near_recv,
    outer_send,
    outer_recv,
    next_send,
    next_recv,
    next_local,
):
    rows, width, lanes = courant.shape
    here = lax.axis_index("depth")
    me = lax.axis_index("shot")
    outer_count = depth_count // inner_count
    inner_me = lax.rem(here, inner_count)
    outer_me = lax.div(here, inner_count)
    piece = width // shot_count
    first = 0
    last = depth_count - 1

    def shot_peer(step):
        return lax.rem(me + step, shot_count)

    def outer_peer(step):
        return lax.rem(outer_me + step, outer_count)

    def depth_of(outer, inner):
        return outer * inner_count + inner

    barrier = pltpu.get_barrier_semaphore()

    def greet(depth, shot):
        pl.semaphore_signal(barrier, inc=1, device_id=(depth, shot), device_id_type=MESH)

    half = shot_count // 2
    order = [
        (turn, flip, chip, core)
        for turn in range(half)
        for flip in range(2)
        for chip in range(inner_count // 2)
        for core in range(2)
    ]
    order.remove((0, 0, 0, 0))

    def hops(offset):
        turn, flip, chip, core = offset
        return min(turn, half - turn) + (1 if flip else 2 * chip) + 0.1 * core

    order.sort(key=hops, reverse=True)

    def near_peer(offset):
        turn, flip, chip, core = offset
        shot = lax.rem(lax.div(me, 2) + turn, half) * 2 + lax.rem(lax.rem(me, 2) + flip, 2)
        inner = lax.rem(lax.div(inner_me, 2) + chip, inner_count // 2) * 2
        inner = inner + lax.rem(lax.rem(inner_me, 2) + core, 2)
        return depth_of(outer_me, inner), shot

    near_peers = [near_peer(offset) for offset in order]
    shot_order = sorted(
        range(1, shot_count),
        key=lambda step: (step % 2 == 0, abs(step - half - (step % 2))),
    )
    turns = sorted(range(1, outer_count), key=lambda turn: -min(turn, outer_count - turn))
    outer_peers = [(depth_of(outer_peer(turn), inner_me), me) for turn in turns]
    greet(lax.rem(here + 1, depth_count), me)
    greet(lax.rem(here + depth_count - 1, depth_count), me)
    for depth, shot in outer_peers + near_peers:
        greet(depth, shot)
    greetings = 2 + len(near_peers) + len(outer_peers)

    inside = pl.ds(REACH, rows)
    across = pl.ds(PAD, width)
    loads = [
        pltpu.make_async_copy(courant_hbm, courant, load_sem.at[0]),
        pltpu.make_async_copy(adjoint_hbm.at[0], adj.at[0], load_sem.at[1]),
        pltpu.make_async_copy(current_hbm.at[0], wave.at[0, inside, across], load_sem.at[2]),
        pltpu.make_async_copy(before_hbm.at[0], before, load_sem.at[3]),
        pltpu.make_async_copy(after_hbm.at[0], after, load_sem.at[4]),
        pltpu.make_async_copy(history_hbm, history, load_sem.at[5]),
        pltpu.make_async_copy(receiver_hbm, receiver_ref, load_sem.at[6]),
        pltpu.make_async_copy(residual_hbm, residual_ref, load_sem.at[7]),
        pltpu.make_async_copy(wavelet_hbm, wavelet_ref, load_sem.at[8]),
    ]
    for load in loads:
        load.start()

    upper = lax.rem(here, 2) == 0

    def by_core(if_upper, if_lower):
        return jnp.where(upper, if_upper, if_lower)

    far_low = by_core(0, rows - REACH)
    most_low = by_core(REACH, 0)
    most = rows - REACH
    far_to = by_core(here - 1, here + 1)
    near_to = by_core(here + 1, here - 1)
    has_far = (far_to >= first) & (far_to <= last)

    def halo_copy(field, number, moment, far, source=None):
        if far:
            start, target = by_core(REACH, rows), by_core(REACH + rows, 0)
        else:
            start, target = by_core(rows, REACH), by_core(0, REACH + rows)
        if source is None:
            source = field.at[moment, pl.ds(start, REACH), across]
        else:
            source = source.at[0, pl.ds(start - REACH, REACH)]
        return pltpu.make_async_remote_copy(
            src_ref=source,
            dst_ref=field.at[moment, pl.ds(target, REACH), across],
            send_sem=halo_send.at[number, moment, 1 if far else 0],
            recv_sem=halo_recv.at[number, moment, 1 if far else 0],
            device_id=(far_to if far else near_to, me),
            device_id_type=MESH,
        )

    def when_far(far, body):
        if far:
            pl.when(has_far)(body)
        else:
            body()

    def send_halo(field, number, moment, far, source=None):
        when_far(far, lambda: halo_copy(field, number, moment, far, source).start())

    def wait_halo(field, number, moment, far):
        when_far(far, lambda: halo_copy(field, number, moment, far).wait_recv())

    pl.semaphore_wait(barrier, greetings)

    send_halo(wave, 0, 0, True, current_hbm)
    send_halo(wave, 0, 0, False, current_hbm)

    pads = jnp.zeros((rows, PAD, lanes), jnp.float32)
    for field in (wave, scaled_adj):
        for moment in range(STEPS):
            field[moment, pl.ds(REACH, rows), pl.ds(0, PAD), :] = pads
            field[moment, pl.ds(REACH, rows), pl.ds(PAD + width, PAD), :] = pads
    outside = jnp.zeros((REACH, width, lanes), jnp.float32)

    @pl.when(here == first)
    def _():
        for field in (wave, scaled_adj):
            for moment in range(STEPS):
                field[moment, pl.ds(0, REACH), across, :] = outside

    @pl.when(here == last)
    def _():
        for field in (wave, scaled_adj):
            for moment in range(STEPS):
                field[moment, pl.ds(REACH + rows, REACH), across, :] = outside

    lane_bits = lanes.bit_length() - 1
    for load in loads[6:]:
        load.wait()
    cells = receiver_ref[...]
    count = cells.shape[1]
    cell_rows = lax.shift_right_logical(cells, lane_bits) - here * (rows * width)
    cell_lanes = cells & (lanes - 1)
    lane_hit = lax.broadcasted_iota(jnp.int32, (lanes, count), 0) == cell_lanes
    block = 4 * width
    weights = []
    for moment in range(STEPS):
        value = jnp.where(lane_hit, residual_ref[0, moment : moment + 1, :], 0.0)
        weights.append(in_three(value))

    def inject_block(number, carry):
        ids = lax.broadcasted_iota(jnp.int32, (block, count), 0) + number * block
        hit = jnp.where(ids == cell_rows, 1.0, 0.0).astype(jnp.bfloat16)
        for moment in range(STEPS):
            total = None
            for weight in reversed(weights[moment]):
                product = lax.dot_general(
                    hit, weight, (((1,), (1,)), ((), ())), preferred_element_type=jnp.float32
                )
                total = product if total is None else total + product
            inject[moment, pl.ds(number * 4, 4)] = total.reshape(4, width, lanes)
        return carry

    lax.fori_loop(0, rows // 4, inject_block, 0)

    loads[0].wait()
    loads[1].wait()

    def first_scaled(z):
        scaled_adj[0, z + REACH, across, :] = courant[z] * adj[0, z]

    def planes(low, count, body):
        def one(number, carry):
            for step in range(BLOCK):
                body(low + BLOCK * number + step)
            return carry

        lax.fori_loop(0, count // BLOCK, one, 0)

    planes(far_low, REACH, first_scaled)
    send_halo(scaled_adj, 1, 0, True)
    planes(most_low, most, first_scaled)
    send_halo(scaled_adj, 1, 0, False)

    source = source_ref[0]
    plane_ids = lax.broadcasted_iota(jnp.int32, (width, lanes), 0) * lanes
    plane_ids = plane_ids + lax.broadcasted_iota(jnp.int32, (width, lanes), 1)

    gap = jnp.abs(
        lax.broadcasted_iota(jnp.int32, (lanes, lanes), 0)
        - lax.broadcasted_iota(jnp.int32, (lanes, lanes), 1)
    )
    weight = jnp.zeros((lanes, lanes), jnp.float32)
    for reach in range(1, REACH + 1):
        weight = jnp.where(gap == reach, float(round(DENOMINATOR * coefficients[reach])), weight)
    weight = weight.astype(jnp.bfloat16)
    for number in range(3):
        band[pl.ds(number * lanes, lanes), :] = weight

    def along(field, moment, low, count):
        value = field[moment, pl.ds(low + REACH, count), across, :].reshape(count * width, lanes)
        split = jnp.concatenate(in_three(value), axis=1)
        product = jnp.dot(split, band[...], preferred_element_type=jnp.float32)
        lateral[pl.ds(low, count)] = product.reshape(count, width, lanes)

    def laplace(field, moment, z):
        at = z + REACH
        center = field[moment, at, across, :]
        total = (3.0 * coefficients[0]) * center + (1.0 / DENOMINATOR) * lateral[z]
        for reach in range(1, REACH + 1):
            depth = field[moment, at + reach, across, :] + field[moment, at - reach, across, :]
            side = (
                field[moment, at, pl.ds(PAD + reach, width), :]
                + field[moment, at, pl.ds(PAD - reach, width), :]
            )
            total = total + coefficients[reach] * (depth + side)
        return center, total

    def forward_plane(moment, z):
        center, total = laplace(wave, moment, z)
        lap[moment, z] = total
        if moment < STEPS - 1:
            old = before[z] if moment == 0 else wave[moment - 1, z + REACH, across, :]
            new = 2.0 * center - old + courant[z] * total
            offset = source - (here * rows + z) * (width * lanes)
            new = new + jnp.where(plane_ids == offset, wavelet_ref[0, moment], 0.0)
            wave[moment + 1, z + REACH, across, :] = new

    def adjoint_plane(moment, z):
        _, total = laplace(scaled_adj, moment, z)
        old = after[z] if moment == 0 else adj[moment - 1, z]
        new = 2.0 * adj[moment, z] - old + total + inject[STEPS - 1 - moment, z]
        if moment < STEPS - 1:
            adj[moment + 1, z] = new
            scaled_adj[moment + 1, z + REACH, across, :] = courant[z] * new
        else:
            total = new * lap[0, z]
            for number in range(1, STEPS):
                total = total + adj[number, z] * lap[STEPS - number, z]
            terms[:, z] = total.reshape(shot_count, piece, lanes)

    stretches = ((most_low, most), (far_low, REACH))

    def part_copy(number, peer, slot):
        start, length = stretches[number]
        return pltpu.make_async_remote_copy(
            src_ref=terms.at[peer, pl.ds(start, length)],
            dst_ref=parts.at[slot, pl.ds(start, length)],
            send_sem=part_send.at[number, peer],
            recv_sem=part_recv.at[number, slot],
            device_id=(here, peer),
            device_id_type=MESH,
        )

    def send_parts(number):
        for step in shot_order:
            part_copy(number, shot_peer(step), me).start()

    def forward(moment, low, count):
        for start in range(0, count, BLOCK):
            along(wave, moment, low + start, BLOCK)
        planes(low, count, functools.partial(forward_plane, moment))

    def adjoint(moment, low, count):
        for start in range(0, count, BLOCK):
            along(scaled_adj, moment, low + start, BLOCK)
        planes(low, count, functools.partial(adjoint_plane, moment))

    loads[2].wait()
    loads[3].wait()
    loads[4].wait()
    for moment in range(STEPS):
        more = moment < STEPS - 1
        wait_halo(wave, 0, moment, False)
        forward(moment, most_low, most)
        if more:
            send_halo(wave, 0, moment + 1, False)
        wait_halo(scaled_adj, 1, moment, False)
        adjoint(moment, most_low, most)
        if more:
            send_halo(scaled_adj, 1, moment + 1, False)
        else:
            send_parts(0)
        wait_halo(wave, 0, moment, True)
        forward(moment, far_low, REACH)
        if more:
            send_halo(wave, 0, moment + 1, True)
        wait_halo(scaled_adj, 1, moment, True)
        adjoint(moment, far_low, REACH)
        if more:
            send_halo(scaled_adj, 1, moment + 1, True)
        else:
            send_parts(1)

    loads[5].wait()
    pairs = [(0, i, j) for j in range(PAIRS) for i in range(j + 1)]
    pairs += [(1, i, j) for j in range(PAIRS) for i in range(j + 1)]

    def gram_plane(z, sums):
        held = [[history[kind, i, z] for i in range(PAIRS)] for kind in range(2)]
        return tuple(
            total + held[kind][i] * held[1][j]
            for total, (kind, i, j) in zip(sums, pairs)
        )

    sums = lax.fori_loop(
        0, rows, gram_plane, tuple(jnp.zeros((piece, lanes), jnp.float32) for _ in pairs)
    )
    row_lane = lax.broadcasted_iota(jnp.int32, (1, lanes), 1)
    packed = jnp.zeros((1, lanes), jnp.float32)
    for total, (kind, i, j) in zip(sums, pairs):
        value = jnp.sum(jnp.sum(total, axis=0, keepdims=True), axis=1, keepdims=True)
        spots = [(2 + PAIRS * kind + j) * 8 + i]
        if kind == 1 and i != j:
            spots.append((2 + PAIRS * kind + i) * 8 + j)
        for spot in spots:
            packed = jnp.where(row_lane == spot, value, packed)
    gram[...] = packed

    for number in range(len(stretches)):
        for step in range(1, shot_count):
            part_copy(number, me, shot_peer(step)).wait_recv()

    scale = 1.0 / (shot_count * STEPS)

    def own_plane(z, sums):
        total = terms[me, z]
        for step in range(1, shot_count):
            total = total + parts[shot_peer(step), z]
        pair_out[0, z] = total
        total = total * scale
        return tuple(
            held + history[number // PAIRS, number % PAIRS, z] * total
            for number, held in enumerate(sums)
        )

    sums = lax.fori_loop(
        0,
        rows,
        own_plane,
        tuple(jnp.zeros((piece, lanes), jnp.float32) for _ in range(2 * PAIRS)),
        unroll=4,
    )
    row_lane = lax.broadcasted_iota(jnp.int32, (1, lanes), 1)
    packed = gram[...]
    for number, total in enumerate(sums):
        value = jnp.sum(jnp.sum(total, axis=0, keepdims=True), axis=1, keepdims=True)
        spot = (number // PAIRS) * 8 + number % PAIRS
        packed = jnp.where(row_lane == spot, value, packed)

    def gather_sum(value, slots, send, recv, mine, peers):
        slots[mine] = value
        for peer in peers:
            pltpu.make_async_remote_copy(
                src_ref=slots.at[mine],
                dst_ref=slots.at[mine],
                send_sem=send,
                recv_sem=recv,
                device_id=peer,
                device_id_type=MESH,
            ).start()
        every = slots.at[pl.ds(0, len(peers))]
        every = pltpu.make_async_remote_copy(
            src_ref=every,
            dst_ref=every,
            send_sem=send,
            recv_sem=recv,
            device_id=peers[0],
            device_id_type=MESH,
        )
        every.wait_recv()
        sums = [slots[slot] for slot in range(len(peers) + 1)]
        while len(sums) > 1:
            sums = [sums[i] + sums[i + 1] for i in range(0, len(sums), 2)]
        return sums[0], every

    near_me = me * inner_count + inner_me
    packed, near_every = gather_sum(packed, slots_near, near_send, near_recv, near_me, near_peers)
    packed, outer_every = gather_sum(packed, slots_outer, outer_send, outer_recv, outer_me, outer_peers)

    spread = jnp.broadcast_to(packed, (8, lanes))
    sub = lax.broadcasted_iota(jnp.int32, (8, lanes), 0)
    lane = lax.broadcasted_iota(jnp.int32, (8, lanes), 1)

    def column(spots):
        return jnp.broadcast_to(
            jnp.sum(jnp.where(lane == spots, spread, 0.0), axis=1, keepdims=True), (8, lanes)
        )

    step_grad = column(sub)
    change_grad = column(8 + sub)
    step_change = [column((2 + j) * 8 + sub) for j in range(PAIRS)]
    step_change_row = [column((2 + sub) * 8 + i) for i in range(PAIRS)]
    change_change = [column((2 + PAIRS + j) * 8 + sub) for j in range(PAIRS)]
    curvature = jnp.where(sub < PAIRS, column((2 + sub) * 8 + sub), 1.0)
    inverse = 1.0 / curvature

    def entry(value, i):
        return jnp.broadcast_to(value[i : i + 1, :], (8, lanes))

    alphas = [None] * PAIRS
    running = step_grad
    for i in reversed(range(PAIRS)):
        alphas[i] = entry(inverse * running, i)
        running = running - alphas[i] * step_change[i]
    gamma = entry(curvature, PAIRS - 1) / entry(change_change[PAIRS - 1], PAIRS - 1)
    running = change_grad
    for j in range(PAIRS):
        running = running - alphas[j] * change_change[j]
    running = gamma * running
    gains = []
    for i in range(PAIRS):
        gain = alphas[i] - entry(inverse * running, i)
        gains.append(gain)
        running = running + gain * step_change_row[i]

    own_lateral = pl.ds(pl.multiple_of(me * piece, piece), piece)

    def direction_plane(z, carry):
        search = pair_out[0, z] * scale
        for i in range(PAIRS):
            search = search - alphas[i] * history[1, i, z]
        search = gamma * search
        for i in range(PAIRS):
            search = search + gains[i] * history[0, i, z]
        pair_out[1, z] = search
        next_piece[z] = courant[z, own_lateral, :] - 0.05 * search
        return carry

    lax.fori_loop(0, rows, direction_plane, 0, unroll=4)

    def next_copy(peer, slot):
        spot = pl.ds(pl.multiple_of(slot * piece, piece), piece)
        return pltpu.make_async_remote_copy(
            src_ref=next_piece,
            dst_ref=next_out.at[:, spot],
            send_sem=next_send.at[peer],
            recv_sem=next_recv.at[slot],
            device_id=(here, peer),
            device_id_type=MESH,
        )

    for step in shot_order:
        next_copy(shot_peer(step), me).start()
    own = pltpu.make_async_copy(next_piece, next_out.at[:, own_lateral], next_local)
    own.start()

    for number, field in enumerate((wave, scaled_adj)):
        for moment in range(STEPS):
            when_far(True, halo_copy(field, number, moment, True).wait_send)
            halo_copy(field, number, moment, False).wait_send()

    for number in range(len(stretches)):
        for step in range(1, shot_count):
            part_copy(number, shot_peer(step), me).wait_send()
    near_every.wait_send()
    outer_every.wait_send()
    own.wait()
    for step in range(1, shot_count):
        next_copy(me, shot_peer(step)).wait_recv()
    for step in range(1, shot_count):
        next_copy(shot_peer(step), me).wait_send()


def per_device(
    courant,
    wave_before,
    wave_current,
    adjoint_after,
    adjoint_current,
    source_cell,
    wavelet,
    receiver_cell,
    residual,
    history,
):
    depth_count = lax.axis_size("depth")
    shot_count = lax.axis_size("shot")
    inner_count = 4
    outer_count = depth_count // inner_count
    rows, width, lanes = courant.shape
    piece = width // shot_count
    f32 = jnp.float32
    slab = (rows, width, lanes)
    padded = (STEPS, rows + 2 * REACH, width + 2 * PAD, lanes)
    vmem = pl.BlockSpec(memory_space=pltpu.VMEM)
    anywhere = pl.BlockSpec(memory_space=pltpu.HBM)
    dma = pltpu.SemaphoreType.DMA
    pair, courant_next = pl.pallas_call(
        functools.partial(kernel, depth_count, shot_count, inner_count),
        out_shape=(
            jax.ShapeDtypeStruct((2, rows, piece, lanes), f32),
            jax.ShapeDtypeStruct(slab, f32),
        ),
        in_specs=[pl.BlockSpec(memory_space=pltpu.SMEM)] + [anywhere] * 9,
        out_specs=(vmem, anywhere),
        scratch_shapes=[
            pltpu.SMEM(wavelet.shape, f32),
            pltpu.VMEM(receiver_cell.shape, jnp.int32),
            pltpu.VMEM(residual.shape, f32),
            pltpu.VMEM(padded, f32),
            pltpu.VMEM(padded, f32),
            pltpu.VMEM((STEPS,) + slab, f32),
            pltpu.VMEM((STEPS,) + slab, f32),
            pltpu.VMEM(slab, f32),
            pltpu.VMEM(slab, f32),
            pltpu.VMEM(slab, f32),
            pltpu.VMEM(history.shape, f32),
            pltpu.VMEM((STEPS,) + slab, f32),
            pltpu.VMEM((shot_count, rows, piece, lanes), f32),
            pltpu.VMEM((shot_count, rows, piece, lanes), f32),
            pltpu.VMEM((1, lanes), f32),
            pltpu.VMEM((rows, piece, lanes), f32),
            pltpu.VMEM((3 * lanes, lanes), jnp.bfloat16),
            pltpu.VMEM(slab, f32),
            pltpu.VMEM((shot_count * inner_count, 1, lanes), f32),
            pltpu.VMEM((outer_count, 1, lanes), f32),
            dma((9,)),
            dma((2, STEPS, 2)),
            dma((2, STEPS, 2)),
            dma((2, shot_count)),
            dma((2, shot_count)),
            dma,
            dma,
            dma,
            dma,
            dma((shot_count,)),
            dma((shot_count,)),
            dma,
        ],
        compiler_params=pltpu.CompilerParams(
            collective_id=0, has_side_effects=True, vmem_limit_bytes=36 * 1024 * 1024
        ),
    )(
        source_cell,
        *(
            pltpu.with_memory_space_constraint(array, pltpu.HBM)
            for array in (
                wavelet,
                receiver_cell,
                residual,
                courant,
                wave_before,
                wave_current,
                adjoint_after,
                adjoint_current,
                history,
            )
        )
    )
    return pair[0] * (1.0 / (shot_count * STEPS)), -pair[1], courant_next


def solution(mesh):
    return jax.shard_map(
        per_device,
        mesh=mesh,
        in_specs=(
            P("depth", None, None),
            P("shot", "depth", None, None),
            P("shot", "depth", None, None),
            P("shot", "depth", None, None),
            P("shot", "depth", None, None),
            P("shot"),
            P("shot", None),
            P("shot", None),
            P("shot", None, None),
            P(None, None, "depth", "shot", None),
        ),
        out_specs=(P("depth", "shot", None), P("depth", "shot", None), P("depth", None, None)),
        check_vma=False,
    )
```
